128 devices in a mesh: ctx: 32 (over y, z, core), head: 4 (over x).
Axes of the slice: x: 4, y: 4, z: 4, core: 2. Of those that a mesh axis runs over, the one named last changes fastest.
Arguments:
- query_rows: bfloat16 [8192, 4096], P('ctx', 'head'), may hold values from -6 to 6
- key_rows: bfloat16 [8192, 4096], P('ctx', 'head')
- value_rows: bfloat16 [8192, 4096], P('ctx', 'head'), may hold values from -6 to 6
- beta: float32 [8192, 32], P('ctx', 'head'), may hold values from 0 to 2
- norm_gain: float32 [128], replicated, may hold values from 0.1 to 1.9
- out_cotangent: bfloat16 [8192, 4096], P('ctx', 'head'), may hold values from -0.125 to 0.125
Outputs:
- attended: bfloat16 [8192, 4096], P('ctx', 'head')
- weight_grad: float32 [4096, 4096], P('ctx', 'head')
The draws below stay inside these ranges and needn't reach their ends.
All inputs are finite; a program needn't handle non-finite values.
Results may differ from the reference program's by a relative error of at most 0.0029.
Values may be sent and summed in bfloat16 or wider, within the bound.
No kernel may reach another device: no remote copies, remote signals or barrier semaphores. Data moves between devices by JAX's collectives and lax.ppermute only.
A program may use at most 128 MiB of HBM per device.

```python
import math
import jax
import jax.numpy as jnp
from jax import lax

D = 4096
FEATURE_WIDTHS = 128
GROUP = 64
TOK_DEV = 256
ATTENTION_UNITS = 32
STEP_TOTAL = 8192


def draw_key_rows(key, part):
    streams = jax.random.split(jax.random.fold_in(key, 11), 3)
    result = jax.random.normal(streams[2], (STEP_TOTAL, ATTENTION_UNITS * FEATURE_WIDTHS))
    return result.astype(jnp.float32).astype(jnp.bfloat16)


def draw_beta(key, part):
    parallel_series = jax.random.split(key, 6)
    blocks = STEP_TOTAL // TOK_DEV
    order = jax.random.permutation(parallel_series[0], ATTENTION_UNITS)
    slow_count = ATTENTION_UNITS // 2
    slow = (order < slow_count).astype(jnp.float32)
    factor = jnp.exp(jax.random.uniform(parallel_series[1], (blocks, ATTENTION_UNITS), minval=math.log(0.5), maxval=math.log(2.0)))
    factor_rows = jnp.repeat(factor, TOK_DEV, axis=0)
    rough = jax.random.uniform(parallel_series[2], (STEP_TOTAL, ATTENTION_UNITS), minval=0.5, maxval=1.5)
    small = FEATURE_WIDTHS / STEP_TOTAL * factor_rows * rough
    slow_beta = 2.0 - small
    fast_beta = jax.random.uniform(parallel_series[3], (STEP_TOTAL, ATTENTION_UNITS), minval=0.3, maxval=1.7)
    mixture_beta_level = slow[None, :] * slow_beta + (1.0 - slow[None, :]) * fast_beta
    beginning_indices = jax.random.randint(parallel_series[4], (3,), 0, STEP_TOTAL - FEATURE_WIDTHS // 4)
    element_place = jnp.arange(STEP_TOTAL)[:, None]
    element_spike = jnp.any((element_place >= beginning_indices[None, :]) & (element_place < beginning_indices[None, :] + FEATURE_WIDTHS // 4), axis=1)
    spike_beta_level = jax.random.uniform(parallel_series[5], (STEP_TOTAL, ATTENTION_UNITS), minval=0.6, maxval=1.4)
    return jnp.where(element_spike[:, None], spike_beta_level, mixture_beta_level).astype(jnp.float32)


def strengthened(array, key, source, target, blocks, factor):
    def block_of(dim):
        return (jnp.arange(array.shape[dim]) // (array.shape[dim] // blocks)).reshape((-1,) + (1,) * (array.ndim - 1 - dim))

    first = jax.random.permutation(key, blocks)[block_of(target)]
    far = (block_of(target) + blocks // 2) % blocks
    return jnp.where((block_of(source) == first) | (block_of(source) == far), factor * array, array)


def block_scale(stream_key, extent, cuts, low, high):
    def one(dim, parts):
        steps = jax.random.uniform(jax.random.fold_in(jax.random.fold_in(stream_key, 6), dim), (parts,), jnp.float32, low / len(cuts), high / len(cuts))
        return jnp.repeat(jnp.exp(steps), extent[dim] // parts).reshape((-1,) + (1,) * (len(extent) - dim - 1))

    gain = one(*cuts[0])
    for cut in cuts[1:]:
        gain = gain * one(*cut)
    return gain


def gaussian(own_key, dims, deviation, limit, cuts=(), held_as=jnp.bfloat16):
    values = jax.random.normal(own_key, dims, jnp.float32) * deviation
    if len(cuts) > 0:
        values = block_scale(own_key, dims, cuts, -0.22, 0.18) * values
    return jnp.clip(values, min=-limit, max=limit).astype(held_as)


def bell_draw_with(rng, dims, deviation, most, shards, heavy, kind=jnp.bfloat16):
    values = deviation * jax.random.normal(rng, dims, jnp.float32)
    if shards:
        values = values * block_scale(rng, dims, shards, -0.22, 0.18)
    return jnp.clip(strengthened(values, jax.random.fold_in(rng, 3), *heavy), -most, most).astype(kind)


def setup_inputs(seed: int = 0) -> dict:
    arg_keys = jax.random.split(jax.random.key(seed), 7)
    query_rows = gaussian(arg_keys[0], (STEP_TOTAL, ATTENTION_UNITS * FEATURE_WIDTHS), 1.0, 6.0, ((0, 32), (1, 4)))
    key_rows = draw_key_rows(jax.random.fold_in(arg_keys[6], 71), 0)
    value_rows = gaussian(arg_keys[2], (STEP_TOTAL, ATTENTION_UNITS * FEATURE_WIDTHS), 1.0, 6.0, ((0, 32), (1, 4)))
    beta = draw_beta(jax.random.fold_in(arg_keys[6], 71), 0)
    norm_gain = jnp.clip(1.0 + 0.18 * jax.random.normal(arg_keys[4], (FEATURE_WIDTHS,), jnp.float32), 0.1, 1.9)
    out_cotangent = bell_draw_with(arg_keys[5], (STEP_TOTAL, D), (STEP_TOTAL ** -0.5), 0.125, ((0, 32), (1, 4)), (0, 1, 32, 2.75))
    return {"query_rows": query_rows, "key_rows": key_rows, "value_rows": value_rows, "beta": beta, "norm_gain": norm_gain, "out_cotangent": out_cotangent}


epsilon = 1e-06
highest = lax.Precision.HIGHEST

def matmul(pattern, former, latter):
    return jnp.einsum(pattern, former, latter, precision=highest, preferred_element_type=jnp.float32)

def unit_lower_inverse(strict_lower):
    negated = -strict_lower
    inverse = jnp.eye(GROUP, dtype=jnp.float32) + negated
    power = negated
    doubling = 2
    while doubling < GROUP:
        power = matmul('...ij,...jk->...ik', power, power)
        inverse = matmul('...ij,...jk->...ik', inverse, jnp.eye(GROUP, dtype=jnp.float32) + power)
        doubling = doubling * 2
    return inverse

def reference(query_rows, key_rows, value_rows, beta, norm_gain, out_cotangent):
    tok_total = query_rows.shape[0]
    heads = beta.shape[1]
    groups = tok_total // GROUP
    lower_mask = jnp.tril(jnp.ones((GROUP, GROUP), jnp.float32), -1)
    causal_mask = jnp.tril(jnp.ones((GROUP, GROUP), jnp.float32))

    def heads_view(block):
        return block.astype(jnp.float32).reshape(GROUP, heads, FEATURE_WIDTHS).transpose(1, 0, 2)

    def advance(state, pieces):
        query_block, key_block, value_block, beta_block = pieces
        query_f = heads_view(query_block)
        key_raw = heads_view(key_block)
        key_unit = key_raw * lax.rsqrt(lax.optimization_barrier(jnp.sum(key_raw * key_raw, axis=-1, keepdims=True)) + epsilon)
        value_f = heads_view(value_block)
        strength = beta_block.T[:, :, None]
        inverse = unit_lower_inverse(lower_mask * (strength * matmul('hid,hjd->hij', key_unit, key_unit)))
        stacked = jnp.concatenate([strength * key_unit, strength * value_f], axis=-1)
        solved = matmul('hij,hjd->hid', inverse, stacked)
        corrected = solved[..., FEATURE_WIDTHS:] - matmul('hcd,hde->hce', solved[..., :FEATURE_WIDTHS], state)
        scores = causal_mask * matmul('hid,hjd->hij', query_f, key_unit)
        mixed = matmul('hcd,hde->hce', query_f, state) + matmul('hij,hje->hie', scores, corrected)
        new_state = state + matmul('hcd,hce->hde', key_unit, corrected)
        mean_square = lax.optimization_barrier(jnp.mean(mixed * mixed, axis=-1, keepdims=True))
        normed = mixed * lax.rsqrt(mean_square + epsilon) * norm_gain
        return (new_state, normed.astype(jnp.bfloat16).transpose(1, 0, 2).reshape(GROUP, heads * FEATURE_WIDTHS))
    start = jnp.zeros((heads, FEATURE_WIDTHS, FEATURE_WIDTHS), jnp.float32)
    pieces = (query_rows.reshape(groups, GROUP, heads * FEATURE_WIDTHS), key_rows.reshape(groups, GROUP, heads * FEATURE_WIDTHS), value_rows.reshape(groups, GROUP, heads * FEATURE_WIDTHS), beta.reshape(groups, GROUP, heads))
    final_state, outputs = lax.scan(advance, start, pieces)
    attended = outputs.reshape(tok_total, heads * FEATURE_WIDTHS)
    weight_grad = jnp.dot(out_cotangent.T, attended, preferred_element_type=jnp.float32)
    return (attended, weight_grad)
```

```python
import jax
import jax.numpy as jnp
from jax import lax
from jax.experimental import pallas as pl
from jax.experimental.pallas import tpu as pltpu
from jax.sharding import Mesh, PartitionSpec as P

F = 128
TOK = 256
HEADS = 8
EPS = 1e-06
f32 = jnp.float32
bf16 = jnp.bfloat16


def split(x):
    h = x.astype(bf16)
    return h, (x - h.astype(f32)).astype(bf16)


def dot(a, b):
    return jnp.dot(a, b, preferred_element_type=f32)


def dot_nt(a, b):
    return lax.dot_general(a, b, (((1,), (1,)), ((), ())), preferred_element_type=f32)


def dot_tn(a, b):
    return lax.dot_general(a, b, (((0,), (0,)), ((), ())), preferred_element_type=f32)


def lhs_of(s):
    return jnp.concatenate(s, axis=1)


def rhs_of(s):
    y = jnp.concatenate(s, axis=1)
    return jnp.concatenate([y, y], axis=0)


def mm(a, b):
    o = dot(lhs_of(a), rhs_of(b))
    return o[:, :F] + o[:, F:]


def mm_all(pairs):
    return [mm(a, b) for a, b in pairs]


def map_product(p, r):
    ph, pl_ = split(p)
    rh, rl = split(r)
    return dot(jnp.concatenate([ph, pl_], axis=1), jnp.concatenate([rh, rh], axis=0)) + dot(ph, rl)


HB = 2


def local_kernel(k_ref, v_ref, b_ref, map_ref, xh_ref, xl_ref, r_ref):
    g = pl.program_id(0)
    beta_all = b_ref[...]
    lane8 = lax.broadcasted_iota(jnp.int32, (TOK, HEADS), 1)
    lane = lax.broadcasted_iota(jnp.int32, (TOK, F), 1)
    row = lax.broadcasted_iota(jnp.int32, (F, F), 0)
    col = lax.broadcasted_iota(jnp.int32, (F, F), 1)
    eye = (row == col).astype(f32)
    strict = row > col
    in16 = jnp.logical_and(strict, (row // 16) == (col // 16))
    in64 = jnp.logical_and((row // 64) == (col // 64), (row // 16) > (col // 16))
    in128 = (row // 64) > (col // 64)

    stat = jnp.zeros((TOK, F), f32)
    ks, rs, bs, kraw = [], [], [], []
    for i in range(HB):
        k = k_ref[:, i * F:(i + 1) * F]
        kf = k.astype(f32)
        r = lax.rsqrt(jnp.sum(kf * kf, axis=-1, keepdims=True) + EPS)
        kf = jnp.where(r > 0.0, kf, 0.0)
        b = jnp.sum(jnp.where(lane8 == g * HB + i, beta_all, 0.0), axis=-1, keepdims=True)
        ks.append(kf)
        kraw.append(kf.astype(bf16))
        rs.append(r)
        bs.append(b)
        stat = jnp.where(lane == 2 * i, r, stat)
        stat = jnp.where(lane == 2 * i + 1, b, stat)
    stat_t = jnp.transpose(stat)
    r_ref[0] = stat_t[0:8, :]

    tiles = []
    cross = []
    for i in range(HB):
        r_row = stat_t[2 * i:2 * i + 1, :]
        br = bs[i] * rs[i]
        k1, k2 = kraw[i][:F], kraw[i][F:]
        g11 = dot_nt(k1, k1)
        g2 = dot_nt(k2, kraw[i])
        a11 = g11 * br[:F] * r_row[:, :F]
        a2 = g2 * br[F:] * r_row
        tiles += [a11, a2[:, F:]]
        cross.append(a2[:, :F])
    n = [jnp.where(in16, a, 0.0) for a in tiles]
    ns = [split(a) for a in n]
    n2 = mm_all(zip(ns, ns))
    n2s = [split(a) for a in n2]
    n4 = mm_all(zip(n2s, n2s))
    q1 = mm_all(zip(ns, n2s))
    n4s = [split(a) for a in n4]
    r1 = [eye - a + b - c for a, b, c in zip(n, n2, q1)]
    n8 = mm_all(zip(n4s, n4s))
    q2 = mm_all(zip([split(a) for a in r1], n4s))
    r2 = [a + b for a, b in zip(r1, q2)]
    q3 = mm_all(zip([split(a) for a in r2], [split(a) for a in n8]))
    d = [a + b for a, b in zip(r2, q3)]
    ds = [split(a) for a in d]
    m = mm_all(zip(ds, [split(jnp.where(in64, a, 0.0)) for a in tiles]))
    ms = [split(a) for a in m]
    m2 = mm_all(zip(ms, ms))
    e = [a + b for a, b in zip(d, mm_all(zip([split(a) for a in m2], ds)))]
    t = [a - b for a, b in zip(e, mm_all(zip(ms, [split(a) for a in e])))]
    ts = [split(a) for a in t]
    u = mm_all(zip([split(jnp.where(in128, a, 0.0)) for a in tiles], ts))
    t = [a - b for a, b in zip(t, mm_all(zip(ts, [split(a) for a in u])))]
    ts = [split(a) for a in t]
    c1 = mm_all(zip([split(a) for a in cross], ts[0::2]))
    t21 = [-a for a in mm_all(zip(ts[1::2], [split(a) for a in c1]))]

    for i in range(HB):
        b_row = stat_t[2 * i + 1:2 * i + 2, :]
        t11h, t11l = split(t[2 * i] * b_row[:, :F])
        t2h, t2l = split(jnp.concatenate([t21[i], t[2 * i + 1]], axis=1) * b_row)
        kn = ks[i] * rs[i]
        knh, knl = split(kn)
        v = v_ref[:, i * F:(i + 1) * F]
        bh = jnp.concatenate([knh, v], axis=1)
        bh1 = bh[:F]
        x1 = dot(jnp.concatenate([t11h, t11l], axis=1), jnp.concatenate([bh1, bh1], axis=0))
        x2 = dot(t2h, bh) + dot(t2l, bh)
        y1 = dot(t11h, knl[:F])
        y2 = dot(t2h, knl)
        x = jnp.concatenate([x1, x2], axis=0)
        y = jnp.concatenate([y1, y2], axis=0)
        x = jnp.concatenate([x[:, :F] + y, x[:, F:]], axis=1)
        xh, xl = split(x)
        xh_ref[i] = xh
        xl_ref[i] = xl
        zh, zl = split(x * rs[i])
        pw = dot_tn(kraw[i], zh) + dot_tn(kraw[i], zl)
        map_ref[i] = jnp.concatenate([eye - pw[:, :F], pw[:, F:]], axis=1)


def local_maps(k, v, beta):
    steps = HEADS // HB
    return pl.pallas_call(
        local_kernel,
        grid=(steps,),
        in_specs=[
            pl.BlockSpec((TOK, HB * F), lambda g: (0, g)),
            pl.BlockSpec((TOK, HB * F), lambda g: (0, g)),
            pl.BlockSpec((TOK, HEADS), lambda g: (0, 0)),
        ],
        out_specs=[
            pl.BlockSpec((HB, F, 2 * F), lambda g: (g, 0, 0)),
            pl.BlockSpec((HB, TOK, 2 * F), lambda g: (g, 0, 0)),
            pl.BlockSpec((HB, TOK, 2 * F), lambda g: (g, 0, 0)),
            pl.BlockSpec((1, 8, TOK), lambda g: (g, 0, 0)),
        ],
        out_shape=[
            jax.ShapeDtypeStruct((HEADS, F, 2 * F), f32),
            jax.ShapeDtypeStruct((HEADS, TOK, 2 * F), bf16),
            jax.ShapeDtypeStruct((HEADS, TOK, 2 * F), bf16),
            jax.ShapeDtypeStruct((steps, 8, TOK), f32),
        ],
        name="local_maps",
    )(k, v, beta)


def reads_kernel(q_ref, k_ref, xh_ref, xl_ref, r_ref, qh_ref, ql_ref, y_ref):
    row = lax.broadcasted_iota(jnp.int32, (TOK, TOK), 0)
    col = lax.broadcasted_iota(jnp.int32, (TOK, TOK), 1)
    causal = row >= col
    for i in range(HB):
        q = q_ref[:, i * F:(i + 1) * F]
        k = k_ref[:, i * F:(i + 1) * F]
        r_row = r_ref[0, 2 * i:2 * i + 1, :]
        s = dot_nt(q, k) * r_row
        s = jnp.where(jnp.logical_and(causal, r_row > 0.0), s, 0.0)
        sh, sl = split(s)
        xh, xl = xh_ref[i], xl_ref[i]
        o = dot(sh, xh) + (dot(sl, xh) + dot(sh, xl))
        qe = q.astype(f32) - o[:, :F]
        qh, ql = split(qe)
        qh_ref[i] = qh
        ql_ref[i] = ql
        y_ref[i] = o[:, F:]


def local_reads(q, k, xh, xl, r):
    steps = HEADS // HB
    per = pl.BlockSpec((HB, TOK, F), lambda g: (g, 0, 0))
    return pl.pallas_call(
        reads_kernel,
        grid=(steps,),
        in_specs=[
            pl.BlockSpec((TOK, HB * F), lambda g: (0, g)),
            pl.BlockSpec((TOK, HB * F), lambda g: (0, g)),
            pl.BlockSpec((HB, TOK, 2 * F), lambda g: (g, 0, 0)),
            pl.BlockSpec((HB, TOK, 2 * F), lambda g: (g, 0, 0)),
            pl.BlockSpec((1, 8, TOK), lambda g: (g, 0, 0)),
        ],
        out_specs=[per, per, per],
        out_shape=[
            jax.ShapeDtypeStruct((HEADS, TOK, F), bf16),
            jax.ShapeDtypeStruct((HEADS, TOK, F), bf16),
            jax.ShapeDtypeStruct((HEADS, TOK, F), f32),
        ],
        name="local_reads",
    )(q, k, xh, xl, r)


def after(p_then, m):
    o = map_product(p_then[:, :F], m)
    return jnp.concatenate([o[:, :F], o[:, F:] + p_then[:, F:]], axis=1)


def scalar_call(kernel, scalar, out_shape, name, *args):
    whole = lambda a: pl.BlockSpec(a.shape, lambda i, s: (0,) * len(a.shape))
    return pl.pallas_call(
        kernel,
        grid_spec=pltpu.PrefetchScalarGridSpec(
            num_scalar_prefetch=1,
            grid=(1,),
            in_specs=[whole(a) for a in args],
            out_specs=jax.tree.map(whole, out_shape),
        ),
        out_shape=out_shape,
        name=name,
    )(scalar.astype(jnp.int32).reshape(1), *args)


def pair_kernel(c_ref, own_ref, got_ref, out_ref):
    c = c_ref[0]
    for j in range(4):
        own = own_ref[4 * c + j]
        got = got_ref[j]
        first = jnp.where(c == 0, own, got)
        second = jnp.where(c == 0, got, own)
        out_ref[j] = after(second, first)


def chain_kernel(z_ref, maps_ref, out_ref):
    m = maps_ref[0]
    out_ref[0] = m
    for j in range(1, 4):
        m = after(maps_ref[j], m)
        out_ref[j] = m


def apply_map(m, s):
    return mm(split(m[:, :F]), split(s)) + m[:, F:]


def plane_kernel(y_ref, m3_ref, m2_ref, m1_ref, pre_ref, out_ref):
    y = y_ref[0]
    s = jnp.where(y >= 3, m3_ref[:, F:], 0.0)
    s = jnp.where(y >= 2, apply_map(m2_ref[...], s), 0.0)
    s = jnp.where(y >= 1, apply_map(m1_ref[...], s), 0.0)
    out_ref[0] = s
    for j in range(3):
        out_ref[j + 1] = apply_map(pre_ref[j], s)


def starts_kernel(c_ref, s_ref, own_ref, got_ref, mine_ref, send_ref):
    c = c_ref[0]
    for j in range(4):
        s = s_ref[j]
        first = jnp.where(c == 0, own_ref[4 * c + j], got_ref[j])
        t = apply_map(first, s)
        mine_ref[j] = jnp.where(c == 0, s, t)
        send_ref[j] = jnp.where(c == 0, t, s)


def out_kernel(c_ref, qh_ref, ql_ref, y_ref, mine_ref, got_ref, g_ref, o_ref):
    h = pl.program_id(0)
    c = c_ref[0]
    for i in range(HB):
        hh = h * HB + i
        j = lax.rem(hh, 4)
        s = jnp.where(lax.div(hh, 4) == c, mine_ref[j], got_ref[j])
        mixed = mm((qh_ref[i], ql_ref[i]), split(s)) + y_ref[i]
        ms = jnp.mean(mixed * mixed, axis=-1, keepdims=True)
        o_ref[:, i * F:(i + 1) * F] = (mixed * lax.rsqrt(ms + EPS) * g_ref[...]).astype(bf16)


def outputs(c, qh, ql, y, mine, got, gain):
    per = pl.BlockSpec((HB, TOK, F), lambda g, s: (g, 0, 0))
    st = pl.BlockSpec((4, F, F), lambda g, s: (0, 0, 0))
    return pl.pallas_call(
        out_kernel,
        grid_spec=pltpu.PrefetchScalarGridSpec(
            num_scalar_prefetch=1,
            grid=(HEADS // HB,),
            in_specs=[per, per, per, st, st, pl.BlockSpec((1, F), lambda g, s: (0, 0))],
            out_specs=pl.BlockSpec((TOK, HB * F), lambda g, s: (0, g)),
        ),
        out_shape=jax.ShapeDtypeStruct((TOK, HEADS * F), bf16),
        name="outputs",
    )(c.astype(jnp.int32).reshape(1), qh, ql, y, mine, got, gain.reshape(1, F))


def shift(x, axis, k):
    return lax.ppermute(x, axis, [(i, (i + k) % 4) for i in range(4)])


def swap(x, axis, k):
    n = 2 if axis == "core" else 4
    return lax.ppermute(x, axis, [(i, i ^ k) for i in range(n)])


def pick(x, i):
    return lax.dynamic_index_in_dim(x, i, 0, False)


def put(x, b, i):
    return lax.dynamic_update_index_in_dim(x, b, i, 0)


def on_device(query_rows, key_rows, value_rows, beta, norm_gain, out_cotangent):
    yi, zi, ci, hi = (lax.axis_index(a) for a in ("y", "z", "core", "head"))

    cot = out_cotangent.reshape(TOK, 4, 2, F)
    cot = jnp.stack([
        lax.dynamic_index_in_dim(cot, 1 - ci, 2, False).reshape(TOK, 4 * F),
        lax.dynamic_index_in_dim(cot, ci, 2, False).reshape(TOK, 4 * F),
    ])
    cot = lax.ppermute(cot, ("y", "head"), [(a * 4 + b, b * 4 + a) for a in range(4) for b in range(4)])
    cots = put(jnp.zeros((4,) + cot.shape, bf16), cot, (yi - hi) % 4)
    for k in (1, 2, 3):
        cots = put(cots, shift(cot, "head", k), (yi - hi + k) % 4)

    maps, xh, xl, r = local_maps(key_rows, value_rows, beta)
    got = swap(lax.dynamic_slice_in_dim(maps, 4 * (1 - ci), 4, 0), "core", 1)
    comb = scalar_call(pair_kernel, ci, jax.ShapeDtypeStruct((4, F, 2 * F), f32), "pair", maps, got)
    chain = put(jnp.zeros_like(comb), pick(comb, zi), zi)
    for k in (1, 2, 3):
        chain = put(chain, shift(pick(comb, (zi + k) % 4), "z", k), (zi - k) % 4)
    qh, ql, yl = local_reads(query_rows, key_rows, xh, xl, r)
    pre = scalar_call(chain_kernel, zi, jax.ShapeDtypeStruct((4, F, 2 * F), f32), "chain", chain)
    m1, m2, m3 = (shift(pre[3], "y", k) for k in (1, 2, 3))
    sc = scalar_call(plane_kernel, yi, jax.ShapeDtypeStruct((4, F, F), f32), "plane", m3, m2, m1, pre)
    sx = put(jnp.zeros_like(sc), pick(sc, zi), zi)
    for k in (1, 2, 3):
        sx = put(sx, shift(pick(sc, (zi + k) % 4), "z", k), (zi - k) % 4)
    half = jax.ShapeDtypeStruct((4, F, F), f32)
    mine, send = scalar_call(starts_kernel, ci, (half, half), "starts", sx, maps, got)
    theirs = swap(send, "core", 1)
    attended = outputs(ci, qh, ql, yl, mine, theirs, norm_gain)

    a_up = shift(attended, "y", 1)
    a_dn = shift(attended, "y", -1)
    h = HEADS * F // 2
    far = jnp.concatenate([shift(a_up[:, :h], "y", 1), shift(a_dn[:, h:], "y", -1)], axis=1)
    att = jnp.concatenate([attended, a_up, far, a_dn], axis=0)
    cs = cots[:, 0].reshape(4 * TOK, 4 * F)
    ck = cots[:, 1].reshape(4 * TOK, 4 * F)
    w_send = dot_tn(cs, att).astype(bf16)
    w_got = swap(w_send, "core", 1)
    w = (dot_tn(ck, att) + w_got.astype(f32)).reshape(4, F, HEADS * F)

    def halving(w, first, second):
        z1, z2, z3 = zi ^ first, zi ^ first ^ second, zi ^ second
        s = swap(jnp.stack([pick(w, z1), pick(w, z2)]).astype(bf16), "z", first).astype(f32)
        keep, on = pick(w, zi) + s[0], pick(w, z3) + s[1]
        return keep + swap(on.astype(bf16), "z", second).astype(f32)

    grad = jnp.concatenate([halving(w[:, :, :h], 1, 3), halving(w[:, :, h:], 3, 1)], axis=1)
    return attended, grad


def solution(mesh):
    fine = Mesh(mesh.devices.reshape(4, 4, 2, 4), ("y", "z", "core", "head"))
    spec = P(("y", "z", "core"), "head")
    return jax.shard_map(
        on_device,
        mesh=fine,
        in_specs=(spec, spec, spec, spec, P(), spec),
        out_specs=(spec, spec),
        check_vma=False,
    )
```

```python
import functools

import jax
import jax.numpy as jnp
from jax import lax
from jax.experimental import pallas as pl
from jax.experimental.pallas import tpu as pltpu
from jax.sharding import Mesh, PartitionSpec as P


F = 128
TOK = 256
HEADS = 8
EPS = 1e-06
f32 = jnp.float32
bf16 = jnp.bfloat16


def split(x):
    h = x.astype(bf16)
    return h, (x - h.astype(f32)).astype(bf16)


def dot(a, b):
    return jnp.dot(a, b, preferred_element_type=f32)


def dot_nt(a, b):
    return lax.dot_general(a, b, (((1,), (1,)), ((), ())), preferred_element_type=f32)


def dot_tn(a, b):
    return lax.dot_general(a, b, (((0,), (0,)), ((), ())), preferred_element_type=f32)


def lhs_of(s):
    return jnp.concatenate(s, axis=1)


def rhs_of(s):
    y = jnp.concatenate(s, axis=1)
    return jnp.concatenate([y, y], axis=0)


def mm(a, b):
    o = dot(lhs_of(a), rhs_of(b))
    return o[:, :F] + o[:, F:]


def mm_all(pairs):
    return [mm(a, b) for a, b in pairs]


def map_product(p, r):
    ph, pl_ = split(p)
    rh, rl = split(r)
    return dot(jnp.concatenate([ph, pl_], axis=1), jnp.concatenate([rh, rh], axis=0)) + dot(ph, rl)


HB = 2


def half_of(mine, w):
    return w[2] if mine else 1 - w[2]


def local_kernel(mine, w_ref, k_ref, v_ref, b_ref, map_ref, xh_ref, xl_ref, r_ref):
    g = pl.program_id(0)
    first_head = half_of(mine, w_ref) * 4 + g * HB
    beta_rows = b_ref[...]
    beta_cols = jnp.transpose(jnp.concatenate([beta_rows, jnp.zeros((F - HEADS, TOK), f32)], axis=0))
    lane = lax.broadcasted_iota(jnp.int32, (TOK, F), 1)
    row = lax.broadcasted_iota(jnp.int32, (F, F), 0)
    col = lax.broadcasted_iota(jnp.int32, (F, F), 1)
    eye = (row == col).astype(f32)
    strict = row > col
    in16 = jnp.logical_and(strict, (row // 16) == (col // 16))
    in64 = jnp.logical_and((row // 64) == (col // 64), (row // 16) > (col // 16))
    in128 = (row // 64) > (col // 64)

    stat = jnp.zeros((TOK, F), f32)
    ks, rs, bs, kraw = [], [], [], []
    for i in range(HB):
        k = k_ref[:, i * F:(i + 1) * F]
        kf = k.astype(f32)
        r = lax.rsqrt(jnp.sum(kf * kf, axis=-1, keepdims=True) + EPS)
        kf = jnp.where(r > 0.0, kf, 0.0)
        b = jnp.sum(jnp.where(lane == first_head + i, beta_cols, 0.0), axis=-1, keepdims=True)
        ks.append(kf)
        kraw.append(kf.astype(bf16))
        rs.append(r)
        bs.append(b)
        stat = jnp.where(lane == 2 * i, r, stat)
        stat = jnp.where(lane == 2 * i + 1, b, stat)
    stat_t = jnp.transpose(stat)
    r_ref[g] = stat_t[0:8, :]

    tiles = []
    cross = []
    for i in range(HB):
        r_row = stat_t[2 * i:2 * i + 1, :]
        br = bs[i] * rs[i]
        k1, k2 = kraw[i][:F], kraw[i][F:]
        g11 = dot_nt(k1, k1)
        g2 = dot_nt(k2, kraw[i])
        a11 = g11 * br[:F] * r_row[:, :F]
        a2 = g2 * br[F:] * r_row
        tiles += [a11, a2[:, F:]]
        cross.append(a2[:, :F])
    n = [jnp.where(in16, a, 0.0) for a in tiles]
    ns = [split(a) for a in n]
    n2 = mm_all(zip(ns, ns))
    n2s = [split(a) for a in n2]
    n4 = mm_all(zip(n2s, n2s))
    q1 = mm_all(zip(ns, n2s))
    n4s = [split(a) for a in n4]
    r1 = [eye - a + b - c for a, b, c in zip(n, n2, q1)]
    n8 = mm_all(zip(n4s, n4s))
    q2 = mm_all(zip([split(a) for a in r1], n4s))
    r2 = [a + b for a, b in zip(r1, q2)]
    q3 = mm_all(zip([split(a) for a in r2], [split(a) for a in n8]))
    d = [a + b for a, b in zip(r2, q3)]
    ds = [split(a) for a in d]
    m = mm_all(zip(ds, [split(jnp.where(in64, a, 0.0)) for a in tiles]))
    ms = [split(a) for a in m]
    m2 = mm_all(zip(ms, ms))
    e = [a + b for a, b in zip(d, mm_all(zip([split(a) for a in m2], ds)))]
    t = [a - b for a, b in zip(e, mm_all(zip(ms, [split(a) for a in e])))]
    ts = [split(a) for a in t]
    u = mm_all(zip([split(jnp.where(in128, a, 0.0)) for a in tiles], ts))
    t = [a - b for a, b in zip(t, mm_all(zip(ts, [split(a) for a in u])))]
    ts = [split(a) for a in t]
    c1 = mm_all(zip([split(a) for a in cross], ts[0::2]))
    t21 = [-a for a in mm_all(zip(ts[1::2], [split(a) for a in c1]))]

    for i in range(HB):
        b_row = stat_t[2 * i + 1:2 * i + 2, :]
        t11h, t11l = split(t[2 * i] * b_row[:, :F])
        t2h, t2l = split(jnp.concatenate([t21[i], t[2 * i + 1]], axis=1) * b_row)
        kn = ks[i] * rs[i]
        knh, knl = split(kn)
        v = v_ref[:, i * F:(i + 1) * F]
        bh = jnp.concatenate([knh, v], axis=1)
        bh1 = bh[:F]
        x1 = dot(jnp.concatenate([t11h, t11l], axis=1), jnp.concatenate([bh1, bh1], axis=0))
        x2 = dot(t2h, bh) + dot(t2l, bh)
        y1 = dot(t11h, knl[:F])
        y2 = dot(t2h, knl)
        x = jnp.concatenate([x1, x2], axis=0)
        y = jnp.concatenate([y1, y2], axis=0)
        x = jnp.concatenate([x[:, :F] + y, x[:, F:]], axis=1)
        xh, xl = split(x)
        xh_ref[g * HB + i] = xh
        xl_ref[g * HB + i] = xl
        zh, zl = split(x * rs[i])
        pw = dot_tn(kraw[i], zh) + dot_tn(kraw[i], zl)
        map_ref[g * HB + i] = jnp.concatenate([eye - pw[:, :F], pw[:, F:]], axis=1)


def vmem(shape, dtype=f32):
    return pltpu.VMEM(shape, dtype)


PARAMS = pltpu.CompilerParams(vmem_limit_bytes=24 << 20)


def in_vmem(x):
    return pltpu.with_memory_space_constraint(x, pltpu.VMEM)


ANYV = pl.BlockSpec(memory_space=pltpu.VMEM)


def local_maps(mine, where, k, v, beta_rows):
    steps = 4 // HB
    cols = pl.BlockSpec((TOK, HB * F), lambda g, w: (0, half_of(mine, w) * steps + g))
    return pl.pallas_call(
        functools.partial(local_kernel, mine),
        grid_spec=pltpu.PrefetchScalarGridSpec(
            num_scalar_prefetch=1,
            grid=(steps,),
            in_specs=[cols, cols, pl.BlockSpec((HEADS, TOK), lambda g, w: (0, 0))],
            out_specs=[ANYV] * 4,
        ),
        out_shape=[
            vmem((4, F, 2 * F)),
            vmem((4, TOK, 2 * F), bf16),
            vmem((4, TOK, 2 * F), bf16),
            vmem((steps, 8, TOK)),
        ],
        compiler_params=PARAMS,
        name="local_maps",
    )(where, k, v, beta_rows)


def reads_kernel(w_ref, q_ref, k_ref, xh_ref, xl_ref, r_ref, m_ref, qh_ref, ql_ref, y_ref):
    g = pl.program_id(0)
    row = lax.broadcasted_iota(jnp.int32, (TOK, TOK), 0)
    col = lax.broadcasted_iota(jnp.int32, (TOK, TOK), 1)
    causal = row >= col
    for i in range(HB):
        q = q_ref[:, i * F:(i + 1) * F]
        k = k_ref[:, i * F:(i + 1) * F]
        r_row = r_ref[g, 2 * i:2 * i + 1, :]
        s = dot_nt(q, k) * r_row
        s = jnp.where(jnp.logical_and(causal, r_row > 0.0), s, 0.0)
        sh, sl = split(s)
        n = g * HB + i
        xh, xl = xh_ref[n], xl_ref[n]
        o = dot(sh, xh) + (dot(sl, xh) + dot(sh, xl))
        qe = q.astype(f32) - o[:, :F]
        qh, ql = split(qe)
        qh_ref[n] = qh
        ql_ref[n] = ql
        y_ref[n] = o[:, F:]

        @pl.when(w_ref[2] == 1)
        def _():
            z = map_product(qe, m_ref[n])
            zh, zl = split(z[:, :F])
            qh_ref[n] = zh
            ql_ref[n] = zl
            y_ref[n] = o[:, F:] + z[:, F:]


def local_reads(mine, where, q, k, xh, xl, r, first):
    steps = 4 // HB
    cols = pl.BlockSpec((TOK, HB * F), lambda g, w: (0, half_of(mine, w) * steps + g))
    return pl.pallas_call(
        reads_kernel,
        grid_spec=pltpu.PrefetchScalarGridSpec(
            num_scalar_prefetch=1,
            grid=(steps,),
            in_specs=[cols, cols] + [ANYV] * 4,
            out_specs=[ANYV] * 3,
        ),
        out_shape=[vmem((4, TOK, F), bf16), vmem((4, TOK, F), bf16), vmem((4, TOK, F))],
        compiler_params=PARAMS,
        name="local_reads",
    )(where, q, k, *[in_vmem(a) for a in (xh, xl, r, first)])


def after(p_then, m):
    o = map_product(p_then[:, :F], m)
    return jnp.concatenate([o[:, :F], o[:, F:] + p_then[:, F:]], axis=1)


def stage(kernel, where, outs, *args, scratch=()):
    return pl.pallas_call(
        kernel,
        in_specs=[pl.BlockSpec(memory_space=pltpu.SMEM)] + [ANYV] * len(args),
        out_specs=[ANYV] * len(outs),
        out_shape=list(outs),
        scratch_shapes=list(scratch),
        compiler_params=PARAMS,
    )(where, *[in_vmem(a) for a in args])


def pair_kernel(w_ref, own_ref, got_ref, *out_refs):
    z, c = w_ref[1], w_ref[2]
    for k in range(4):
        j = lax.rem(z + k, 4)
        own = own_ref[j]
        got = got_ref[j]
        out_refs[k][...] = after(jnp.where(c == 0, got, own), jnp.where(c == 0, own, got))


def chain_kernel(w_ref, m0_ref, m1_ref, m2_ref, m3_ref, pre_ref, all_ref, maps_ref):
    z = w_ref[1]
    for k, ref in enumerate((m0_ref, m1_ref, m2_ref, m3_ref)):
        maps_ref[lax.rem(z - k + 4, 4)] = ref[...]
    m = maps_ref[0]
    pre_ref[0] = m
    for j in range(1, 4):
        m = after(maps_ref[j], m)
        if j < 3:
            pre_ref[j] = m
    all_ref[...] = m


def apply_map(m, s):
    return mm(split(m[:, :F]), split(s)) + m[:, F:]


def plane_kernel(w_ref, m3_ref, m2_ref, m1_ref, pre_ref, *out_refs):
    y, z = w_ref[0], w_ref[1]
    s = jnp.where(y >= 3, m3_ref[:, F:], 0.0)
    s = jnp.where(y >= 2, apply_map(m2_ref[...], s), 0.0)
    s = jnp.where(y >= 1, apply_map(m1_ref[...], s), 0.0)
    for k in range(4):
        j = lax.rem(z + k, 4)
        t = apply_map(pre_ref[jnp.maximum(j - 1, 0)], s)
        out_refs[k][...] = jnp.where(j == 0, s, t)


def order_kernel(w_ref, s0_ref, s1_ref, s2_ref, s3_ref, out_ref):
    z = w_ref[1]
    for k, ref in enumerate((s0_ref, s1_ref, s2_ref, s3_ref)):
        out_ref[lax.rem(z - k + 4, 4)] = ref[...]


def out_kernel(w_ref, qh_ref, ql_ref, y_ref, s_ref, g_ref, o_ref):
    mixed = [mm((qh_ref[i], ql_ref[i]), split(s_ref[i])) + y_ref[i] for i in range(4)]
    for i, m in enumerate(mixed):
        ms = jnp.mean(m * m, axis=-1, keepdims=True)
        o_ref[:, i * F:(i + 1) * F] = (m * lax.rsqrt(ms + EPS) * g_ref[...]).astype(bf16)


def outputs(where, qh, ql, y, s, gain):
    return stage(out_kernel, where, [vmem((TOK, 4 * F), bf16)], qh, ql, y, s, gain)[0]


def shift(x, axis, k):
    return lax.ppermute(x, axis, [(i, (i + k) % 4) for i in range(4)])


def swap(x, axis, k):
    n = 2 if axis == "core" else 4
    return lax.ppermute(x, axis, [(i, i ^ k) for i in range(n)])


def pick(x, i):
    return lax.dynamic_index_in_dim(x, i, 0, False)


def body(query_rows, key_rows, value_rows, beta, norm_gain, out_cotangent):
    yi, zi, ci, hi = (lax.axis_index(a).astype(jnp.int32) for a in ("y", "z", "core", "head"))
    where = jnp.stack([yi, zi, ci, hi])

    cot = lax.ppermute(out_cotangent, ("y", "head"), [(a * 4 + b, b * 4 + a) for a in range(4) for b in range(4)])
    cots = [cot]
    for k in (1, 2, 3):
        cots.append(shift(cot, "head", k))
    gain = norm_gain.reshape(1, F)
    beta_rows = beta.T
    m_a, xh_a, xl_a, r_a = local_maps(False, where, key_rows, value_rows, beta_rows)
    got_b = swap(m_a, "core", 1)
    m_b, xh_b, xl_b, r_b = local_maps(True, where, key_rows, value_rows, beta_rows)
    got_a = swap(m_b, "core", 1)
    m4 = vmem((F, 2 * F))
    comb = stage(pair_kernel, where, [m4] * 4, m_b, got_b)
    got = [comb[0]]
    for k in (1, 2, 3):
        got.append(shift(comb[k], "z", k))
    rd_b = local_reads(True, where, query_rows, key_rows, xh_b, xl_b, r_b, got_b)
    rd_a = local_reads(False, where, query_rows, key_rows, xh_a, xl_a, r_a, got_a)
    pre, total = stage(chain_kernel, where, [vmem((3, F, 2 * F)), m4], *got, scratch=[pltpu.VMEM((4, F, 2 * F), f32)])
    planes = []
    for k in (3, 2, 1):
        planes.append(shift(total, "y", k))
    sc = stage(plane_kernel, where, [vmem((F, F))] * 4, *planes, pre)
    sx = [sc[0]]
    for k in (1, 2, 3):
        sx.append(shift(sc[k], "z", k))
    s_b, = stage(order_kernel, where, [vmem((4, F, F))], *sx)
    s_a = swap(s_b, "core", 1)
    att_b = outputs(where, *rd_b, s_b, gain)
    up_b = shift(att_b, "y", 1)
    dn_b = shift(att_b, "y", -1)
    att_a = outputs(where, *rd_a, s_a, gain)
    up_a = shift(att_a, "y", 1)
    dn_a = shift(att_a, "y", -1)
    far_b = shift(up_b, "y", 1)
    far_a = shift(dn_a, "y", -1)

    cots = jnp.stack(cots)
    parts = stage(part_kernel, where, [vmem((4 * F, 8 * F))] * 2, cots, att_b, att_a, up_b, up_a, dn_b, dn_a)
    w_send, = stage(functools.partial(last_kernel, 0), where, [vmem((4 * F, 8 * F), bf16)], cots, far_b, far_a, parts[0])
    w_got = swap(w_send, "core", 1)
    w, = stage(functools.partial(last_kernel, 1), where, [vmem((4 * F, 8 * F))], cots, far_b, far_a, parts[1])
    h = 4 * F
    w_b = (w[:, :h] + w_got[:, h:].astype(f32)).reshape(4, F, h)
    w_a = (w[:, h:] + w_got[:, :h].astype(f32)).reshape(4, F, h)

    def halving(w, first, second):
        z1, z2, z3 = zi ^ first, zi ^ first ^ second, zi ^ second
        s = swap(jnp.concatenate([pick(w, z1), pick(w, z2)]).astype(bf16), "z", first).astype(f32)
        keep, on = pick(w, zi) + s[:F], pick(w, z3) + s[F:]
        return keep + swap(on.astype(bf16), "z", second).astype(f32)

    g_b = halving(w_b, 1, 3)
    g_a = halving(w_a, 3, 1)
    grad = jnp.where(ci == 0, jnp.concatenate([g_b, g_a], axis=1), jnp.concatenate([g_a, g_b], axis=1))
    attended = jnp.where(ci == 0, jnp.concatenate([att_b, att_a], axis=1), jnp.concatenate([att_a, att_b], axis=1))
    return attended, grad


def cot_rows(w_ref, cot_ref, k, part):
    j = lax.rem(w_ref[3] - w_ref[0] + k + 4, 4)
    core = half_of(part == 1, w_ref)
    return jnp.concatenate(
        [cot_ref[j, :, pl.ds(pl.multiple_of((2 * n + core) * F, F), F)] for n in range(4)], axis=1
    )


def part_kernel(w_ref, cot_ref, *refs):
    for s in range(2):
        rows = jnp.concatenate([cot_rows(w_ref, cot_ref, k, s) for k in (0, 1, 3)], axis=0)
        for n in range(2):
            tall = jnp.concatenate([refs[n][...], refs[2 + n][...], refs[4 + n][...]], axis=0)
            refs[6 + s][:, n * 4 * F:(n + 1) * 4 * F] = dot_tn(rows, tall)


def last_kernel(s, w_ref, cot_ref, b_ref, a_ref, part_ref, out_ref):
    rows = cot_rows(w_ref, cot_ref, 2, s)
    for n, ref in enumerate((b_ref, a_ref)):
        cols = slice(n * 4 * F, (n + 1) * 4 * F)
        out_ref[:, cols] = (part_ref[:, cols] + dot_tn(rows, ref[...])).astype(out_ref.dtype)


def solution(mesh):
    fine = Mesh(mesh.devices.reshape(4, 4, 2, 4), ("y", "z", "core", "head"))
    spec = P(("y", "z", "core"), "head")
    return jax.shard_map(
        body,
        mesh=fine,
        in_specs=(spec, spec, spec, spec, P(), spec),
        out_specs=(spec, spec),
        check_vma=False,
    )
```

```python
import functools

import jax
import jax.numpy as jnp
from jax import lax
from jax.experimental import pallas as pl
from jax.experimental.pallas import tpu as pltpu
from jax.sharding import Mesh, PartitionSpec as P


F = 128
TOK = 256
HEADS = 8
EPS = 1e-06
f32 = jnp.float32
bf16 = jnp.bfloat16


def split(x):
    h = x.astype(bf16)
    return h, (x - h.astype(f32)).astype(bf16)


def dot(a, b):
    return jnp.dot(a, b, preferred_element_type=f32)


def dot_nt(a, b):
    return lax.dot_general(a, b, (((1,), (1,)), ((), ())), preferred_element_type=f32)


def dot_tn(a, b):
    return lax.dot_general(a, b, (((0,), (0,)), ((), ())), preferred_element_type=f32)


def lhs_of(s):
    return jnp.concatenate(s, axis=1)


def rhs_of(s):
    y = jnp.concatenate(s, axis=1)
    return jnp.concatenate([y, y], axis=0)


def mm(a, b):
    o = dot(lhs_of(a), rhs_of(b))
    return o[:, :F] + o[:, F:]


def mm_all(pairs):
    return [mm(a, b) for a, b in pairs]


def map_product(p, r):
    ph, pl_ = split(p)
    rh, rl = split(r)
    return dot(jnp.concatenate([ph, pl_], axis=1), jnp.concatenate([rh, rh], axis=0)) + dot(ph, rl)


HB = 4


def half_of(mine, w):
    return w[2] if mine else 1 - w[2]


def local_kernel(mine, w_ref, k_ref, v_ref, b_ref, map_ref, xh_ref, xl_ref, r_ref):
    g = pl.program_id(0)
    first_head = half_of(mine, w_ref) * 4 + g * HB
    beta_rows = b_ref[...]
    beta_cols = jnp.transpose(jnp.concatenate([beta_rows, jnp.zeros((F - HEADS, TOK), f32)], axis=0))
    lane = lax.broadcasted_iota(jnp.int32, (TOK, F), 1)
    row = lax.broadcasted_iota(jnp.int32, (F, F), 0)
    col = lax.broadcasted_iota(jnp.int32, (F, F), 1)
    eye = (row == col).astype(f32)
    strict = row > col
    in16 = jnp.logical_and(strict, (row // 16) == (col // 16))
    in64 = jnp.logical_and((row // 64) == (col // 64), (row // 16) > (col // 16))
    in128 = (row // 64) > (col // 64)

    stat = jnp.zeros((TOK, F), f32)
    ks, rs, bs, kraw = [], [], [], []
    for i in range(HB):
        k = k_ref[:, i * F:(i + 1) * F]
        kf = k.astype(f32)
        r = lax.rsqrt(jnp.sum(kf * kf, axis=-1, keepdims=True) + EPS)
        kf = jnp.where(r > 0.0, kf, 0.0)
        b = jnp.sum(jnp.where(lane == first_head + i, beta_cols, 0.0), axis=-1, keepdims=True)
        ks.append(kf)
        kraw.append(kf.astype(bf16))
        rs.append(r)
        bs.append(b)
        stat = jnp.where(lane == 2 * i, r, stat)
        stat = jnp.where(lane == 2 * i + 1, b, stat)
    stat_t = jnp.transpose(stat)
    r_ref[g] = stat_t[0:8, :]

    tiles = []
    cross = []
    for i in range(HB):
        r_row = stat_t[2 * i:2 * i + 1, :]
        br = bs[i] * rs[i]
        k1, k2 = kraw[i][:F], kraw[i][F:]
        g11 = dot_nt(k1, k1)
        g2 = dot_nt(k2, kraw[i])
        a11 = g11 * br[:F] * r_row[:, :F]
        a2 = g2 * br[F:] * r_row
        tiles += [a11, a2[:, F:]]
        cross.append(a2[:, :F])
    n = [jnp.where(in16, a, 0.0) for a in tiles]
    ns = [split(a) for a in n]
    n2 = mm_all(zip(ns, ns))
    n2s = [split(a) for a in n2]
    n4 = mm_all(zip(n2s, n2s))
    q1 = mm_all(zip(ns, n2s))
    n4s = [split(a) for a in n4]
    r1 = [eye - a + b - c for a, b, c in zip(n, n2, q1)]
    n8 = mm_all(zip(n4s, n4s))
    q2 = mm_all(zip([split(a) for a in r1], n4s))
    r2 = [a + b for a, b in zip(r1, q2)]
    q3 = mm_all(zip([split(a) for a in r2], [split(a) for a in n8]))
    d = [a + b for a, b in zip(r2, q3)]
    ds = [split(a) for a in d]
    m = mm_all(zip(ds, [split(jnp.where(in64, a, 0.0)) for a in tiles]))
    ms = [split(a) for a in m]
    m2 = mm_all(zip(ms, ms))
    e = [a + b for a, b in zip(d, mm_all(zip([split(a) for a in m2], ds)))]
    t = [a - b for a, b in zip(e, mm_all(zip(ms, [split(a) for a in e])))]
    ts = [split(a) for a in t]
    u = mm_all(zip([split(jnp.where(in128, a, 0.0)) for a in tiles], ts))
    t = [a - b for a, b in zip(t, mm_all(zip(ts, [split(a) for a in u])))]
    ts = [split(a) for a in t]
    c1 = mm_all(zip([split(a) for a in cross], ts[0::2]))
    t21 = [-a for a in mm_all(zip(ts[1::2], [split(a) for a in c1]))]

    for i in range(HB):
        b_row = stat_t[2 * i + 1:2 * i + 2, :]
        t11h, t11l = split(t[2 * i] * b_row[:, :F])
        t2h, t2l = split(jnp.concatenate([t21[i], t[2 * i + 1]], axis=1) * b_row)
        kn = ks[i] * rs[i]
        knh, knl = split(kn)
        v = v_ref[:, i * F:(i + 1) * F]
        bh = jnp.concatenate([knh, v], axis=1)
        bh1 = bh[:F]
        x1 = dot(jnp.concatenate([t11h, t11l], axis=1), jnp.concatenate([bh1, bh1], axis=0))
        x2 = dot(t2h, bh) + dot(t2l, bh)
        y1 = dot(t11h, knl[:F])
        y2 = dot(t2h, knl)
        x = jnp.concatenate([x1, x2], axis=0)
        y = jnp.concatenate([y1, y2], axis=0)
        x = jnp.concatenate([x[:, :F] + y, x[:, F:]], axis=1)
        xh, xl = split(x)
        xh_ref[g * HB + i] = xh
        xl_ref[g * HB + i] = xl
        zh, zl = split(x * rs[i])
        pw = dot_tn(kraw[i], zh) + dot_tn(kraw[i], zl)
        map_ref[g * HB + i] = jnp.concatenate([eye - pw[:, :F], pw[:, F:]], axis=1)


def vmem(shape, dtype=f32):
    return pltpu.VMEM(shape, dtype)


PARAMS = pltpu.CompilerParams(vmem_limit_bytes=24 << 20)


def in_hbm(x):
    return pltpu.with_memory_space_constraint(x, pltpu.HBM)


def in_vmem(x):
    return pltpu.with_memory_space_constraint(x, pltpu.VMEM)


ANYV = pl.BlockSpec(memory_space=pltpu.VMEM)


def local_maps(mine, where, k, v, beta_rows):
    steps = 4 // HB
    cols = pl.BlockSpec((TOK, HB * F), lambda g, w: (0, half_of(mine, w) * steps + g))
    return pl.pallas_call(
        functools.partial(local_kernel, mine),
        grid_spec=pltpu.PrefetchScalarGridSpec(
            num_scalar_prefetch=1,
            grid=(steps,),
            in_specs=[cols, cols, pl.BlockSpec((HEADS, TOK), lambda g, w: (0, 0))],
            out_specs=[ANYV] * 4,
        ),
        out_shape=[
            vmem((4, F, 2 * F)),
            vmem((4, TOK, 2 * F), bf16),
            vmem((4, TOK, 2 * F), bf16),
            vmem((steps, 8, TOK)),
        ],
        compiler_params=PARAMS,
        name="local_maps",
    )(where, in_hbm(k), in_hbm(v), in_hbm(beta_rows))


def reads_kernel(w_ref, q_ref, k_ref, xh_ref, xl_ref, r_ref, m_ref, qh_ref, ql_ref, y_ref):
    g = pl.program_id(0)
    row = lax.broadcasted_iota(jnp.int32, (TOK, TOK), 0)
    col = lax.broadcasted_iota(jnp.int32, (TOK, TOK), 1)
    causal = row >= col
    for i in range(HB):
        q = q_ref[:, i * F:(i + 1) * F]
        k = k_ref[:, i * F:(i + 1) * F]
        r_row = r_ref[g, 2 * i:2 * i + 1, :]
        s = dot_nt(q, k) * r_row
        s = jnp.where(jnp.logical_and(causal, r_row > 0.0), s, 0.0)
        sh, sl = split(s)
        n = g * HB + i
        xh, xl = xh_ref[n], xl_ref[n]
        o = dot(sh, xh) + (dot(sl, xh) + dot(sh, xl))
        qe = q.astype(f32) - o[:, :F]
        qh, ql = split(qe)
        qh_ref[n] = qh
        ql_ref[n] = ql
        y_ref[n] = o[:, F:]

        @pl.when(w_ref[2] == 1)
        def _():
            z = map_product(qe, m_ref[n])
            zh, zl = split(z[:, :F])
            qh_ref[n] = zh
            ql_ref[n] = zl
            y_ref[n] = o[:, F:] + z[:, F:]


def local_reads(mine, where, q, k, xh, xl, r, first):
    steps = 4 // HB
    cols = pl.BlockSpec((TOK, HB * F), lambda g, w: (0, half_of(mine, w) * steps + g))
    return pl.pallas_call(
        reads_kernel,
        grid_spec=pltpu.PrefetchScalarGridSpec(
            num_scalar_prefetch=1,
            grid=(steps,),
            in_specs=[cols, cols] + [ANYV] * 4,
            out_specs=[ANYV] * 3,
        ),
        out_shape=[vmem((4, TOK, F), bf16), vmem((4, TOK, F), bf16), vmem((4, TOK, F))],
        compiler_params=PARAMS,
        name="local_reads",
    )(where, in_hbm(q), in_hbm(k), *[in_vmem(a) for a in (xh, xl, r, first)])


def after(p_then, m):
    o = map_product(p_then[:, :F], m)
    return jnp.concatenate([o[:, :F], o[:, F:] + p_then[:, F:]], axis=1)


def stage(kernel, where, outs, *args, scratch=()):
    return pl.pallas_call(
        kernel,
        in_specs=[pl.BlockSpec(memory_space=pltpu.SMEM)] + [ANYV] * len(args),
        out_specs=[ANYV] * len(outs),
        out_shape=list(outs),
        scratch_shapes=list(scratch),
        compiler_params=PARAMS,
    )(where, *[in_vmem(a) for a in args])


def pair_kernel(w_ref, own_ref, got_ref, *out_refs):
    z, c = w_ref[1], w_ref[2]
    for k in range(4):
        j = lax.rem(z + k, 4)
        own = own_ref[j]
        got = got_ref[j]
        out_refs[k][...] = after(jnp.where(c == 0, got, own), jnp.where(c == 0, own, got))


def chain_kernel(w_ref, m0_ref, m1_ref, m2_ref, m3_ref, pre_ref, all_ref, maps_ref):
    z = w_ref[1]
    for k, ref in enumerate((m0_ref, m1_ref, m2_ref, m3_ref)):
        maps_ref[lax.rem(z - k + 4, 4)] = ref[...]
    m = maps_ref[0]
    pre_ref[0] = m
    for j in range(1, 4):
        m = after(maps_ref[j], m)
        if j < 3:
            pre_ref[j] = m
    all_ref[...] = m


def apply_map(m, s):
    return mm(split(m[:, :F]), split(s)) + m[:, F:]


def plane_kernel(w_ref, m3_ref, m2_ref, m1_ref, pre_ref, *out_refs):
    y, z = w_ref[0], w_ref[1]
    s = jnp.where(y >= 3, m3_ref[:, F:], 0.0)
    s = jnp.where(y >= 2, apply_map(m2_ref[...], s), 0.0)
    s = jnp.where(y >= 1, apply_map(m1_ref[...], s), 0.0)
    for k in range(4):
        j = lax.rem(z + k, 4)
        t = apply_map(pre_ref[jnp.maximum(j - 1, 0)], s)
        out_refs[k][...] = jnp.where(j == 0, s, t)


def order_kernel(w_ref, s0_ref, s1_ref, s2_ref, s3_ref, out_ref):
    z = w_ref[1]
    for k, ref in enumerate((s0_ref, s1_ref, s2_ref, s3_ref)):
        out_ref[lax.rem(z - k + 4, 4)] = ref[...]


def out_kernel(w_ref, qh_ref, ql_ref, y_ref, s_ref, g_ref, o_ref):
    mixed = [mm((qh_ref[i], ql_ref[i]), split(s_ref[i])) + y_ref[i] for i in range(4)]
    for i, m in enumerate(mixed):
        ms = jnp.mean(m * m, axis=-1, keepdims=True)
        o_ref[:, i * F:(i + 1) * F] = (m * lax.rsqrt(ms + EPS) * g_ref[...]).astype(bf16)


def outputs(where, qh, ql, y, s, gain):
    return stage(out_kernel, where, [vmem((TOK, 4 * F), bf16)], qh, ql, y, s, gain)[0]


def shift(x, axis, k):
    return lax.ppermute(x, axis, [(i, (i + k) % 4) for i in range(4)])


def swap(x, axis, k):
    n = 2 if axis == "core" else 4
    return lax.ppermute(x, axis, [(i, i ^ k) for i in range(n)])


def body(query_rows, key_rows, value_rows, beta, norm_gain, out_cotangent):
    yi, zi, ci, hi = (lax.axis_index(a).astype(jnp.int32) for a in ("y", "z", "core", "head"))
    where = jnp.stack([yi, zi, ci, hi])

    cot = lax.ppermute(out_cotangent, ("y", "head"), [(a * 4 + b, b * 4 + a) for a in range(4) for b in range(4)])
    cot2 = jnp.stack([cot, swap(cot, "head", 1)])
    cots = jnp.concatenate([cot2, swap(cot2, "head", 3)])
    gain = norm_gain.reshape(1, F)
    beta_rows = beta.T
    m_a, xh_a, xl_a, r_a = local_maps(False, where, key_rows, value_rows, beta_rows)
    got_b = swap(m_a, "core", 1)
    m_b, xh_b, xl_b, r_b = local_maps(True, where, key_rows, value_rows, beta_rows)
    got_a = swap(m_b, "core", 1)
    m4 = vmem((F, 2 * F))
    comb = stage(pair_kernel, where, [m4] * 4, m_b, got_b)
    got = [comb[0]]
    for k in (1, 2, 3):
        got.append(shift(comb[k], "z", k))
    rd_b = local_reads(True, where, query_rows, key_rows, xh_b, xl_b, r_b, got_b)
    rd_a = local_reads(False, where, query_rows, key_rows, xh_a, xl_a, r_a, got_a)
    pre, total = stage(chain_kernel, where, [vmem((3, F, 2 * F)), m4], *got, scratch=[pltpu.VMEM((4, F, 2 * F), f32)])
    planes = []
    for k in (3, 2, 1):
        planes.append(shift(total, "y", k))
    sc = stage(plane_kernel, where, [vmem((F, F))] * 4, *planes, pre)
    sx = [sc[0]]
    for k in (1, 2, 3):
        sx.append(shift(sc[k], "z", k))
    s_b, = stage(order_kernel, where, [vmem((4, F, F))], *sx)
    s_a = swap(s_b, "core", 1)
    att_b = outputs(where, *rd_b, s_b, gain)
    up_b = shift(att_b, "y", 1)
    dn_b = shift(att_b, "y", -1)
    att_a = outputs(where, *rd_a, s_a, gain)
    up_a = shift(att_a, "y", 1)
    dn_a = shift(att_a, "y", -1)
    far_b = shift(up_b, "y", 1)
    far_a = shift(dn_a, "y", -1)

    parts = stage(part_kernel, where, [vmem((4 * F, 8 * F))] * 2, cots, att_b, att_a, up_b, up_a, dn_b, dn_a)
    w_send, = stage(functools.partial(last_kernel, 0), where, [vmem((4 * F, 8 * F), bf16)], cots, far_b, far_a, parts[0])
    w_got = swap(w_send, "core", 1)
    w, = stage(functools.partial(last_kernel, 1), where, [vmem((4 * F, 8 * F))], cots, far_b, far_a, parts[1])
    quarter = vmem((2 * F, 4 * F), bf16)
    kept = vmem((2 * F, 4 * F))
    on_b, on_a, k_b, k_a = stage(sum_kernel, where, [quarter, quarter, kept, kept], w, w_got)
    r_b = swap(on_b, "z", 1)
    r_a = swap(on_a, "z", 3)
    h_b = (k_b[F:] + r_b[F:].astype(f32)).astype(bf16)
    e_b = swap(h_b, "z", 3)
    h_a = (k_a[F:] + r_a[F:].astype(f32)).astype(bf16)
    e_a = swap(h_a, "z", 1)
    grad, = stage(final_kernel, where, [jax.ShapeDtypeStruct((F, 8 * F), f32)], k_b, r_b, e_b, k_a, r_a, e_a)
    attended = jnp.where(ci == 0, jnp.concatenate([att_b, att_a], axis=1), jnp.concatenate([att_a, att_b], axis=1))
    return attended, grad


def cot_rows(w_ref, cot_ref, k, part):
    d = lax.rem(w_ref[0] - k + 4, 4) ^ w_ref[3]
    j = d ^ (d >> 1)
    core = half_of(part == 1, w_ref)
    return jnp.concatenate(
        [cot_ref[j, :, pl.ds(pl.multiple_of((2 * n + core) * F, F), F)] for n in range(4)], axis=1
    )


def part_kernel(w_ref, cot_ref, *refs):
    for s in range(2):
        rows = jnp.concatenate([cot_rows(w_ref, cot_ref, k, s) for k in (0, 1, 3)], axis=0)
        for n in range(2):
            tall = jnp.concatenate([refs[n][...], refs[2 + n][...], refs[4 + n][...]], axis=0)
            refs[6 + s][:, n * 4 * F:(n + 1) * 4 * F] = dot_tn(rows, tall)


def last_kernel(s, w_ref, cot_ref, b_ref, a_ref, part_ref, out_ref):
    rows = cot_rows(w_ref, cot_ref, 2, s)
    for n, ref in enumerate((b_ref, a_ref)):
        cols = slice(n * 4 * F, (n + 1) * 4 * F)
        out_ref[:, cols] = (part_ref[:, cols] + dot_tn(rows, ref[...])).astype(out_ref.dtype)


def sum_kernel(w_ref, keep_ref, got_ref, on_b_ref, on_a_ref, k_b_ref, k_a_ref):
    z = w_ref[1]
    h = 4 * F
    for n, (on_ref, k_ref, first, second) in enumerate(((on_b_ref, k_b_ref, 1, 3), (on_a_ref, k_a_ref, 3, 1))):
        mine = slice(n * h, (n + 1) * h)
        theirs = slice((1 - n) * h, (2 - n) * h)
        for i, (ref, blk) in enumerate(((on_ref, z ^ first), (on_ref, z ^ 2), (k_ref, z), (k_ref, z ^ second))):
            rows = pl.ds(pl.multiple_of(blk * F, F), F)
            total = keep_ref[rows, mine] + got_ref[rows, theirs].astype(f32)
            ref[(i % 2) * F:(i % 2 + 1) * F, :] = total.astype(ref.dtype)


def final_kernel(w_ref, k_b_ref, r_b_ref, e_b_ref, k_a_ref, r_a_ref, e_a_ref, out_ref):
    c = w_ref[2]
    g_b = k_b_ref[:F] + r_b_ref[:F].astype(f32) + e_b_ref[...].astype(f32)
    g_a = k_a_ref[:F] + r_a_ref[:F].astype(f32) + e_a_ref[...].astype(f32)
    h = 4 * F
    out_ref[:, :h] = jnp.where(c == 0, g_b, g_a)
    out_ref[:, h:] = jnp.where(c == 0, g_a, g_b)


def solution(mesh):
    fine = Mesh(mesh.devices.reshape(4, 4, 2, 4), ("y", "z", "core", "head"))
    spec = P(("y", "z", "core"), "head")
    return jax.shard_map(
        body,
        mesh=fine,
        in_specs=(spec, spec, spec, spec, P(), spec),
        out_specs=(spec, spec),
        check_vma=False,
    )
```

```python
import functools

import jax
import jax.numpy as jnp
from jax import lax
from jax.experimental import pallas as pl
from jax.experimental.pallas import tpu as pltpu
from jax.sharding import Mesh, PartitionSpec as P


F = 128
TOK = 256
HEADS = 8
EPS = 1e-06
f32 = jnp.float32
bf16 = jnp.bfloat16


def split(x):
    h = x.astype(bf16)
    return h, (x - h.astype(f32)).astype(bf16)


def dot(a, b):
    return jnp.dot(a, b, preferred_element_type=f32)


def dot_nt(a, b):
    return lax.dot_general(a, b, (((1,), (1,)), ((), ())), preferred_element_type=f32)


def dot_tn(a, b):
    return lax.dot_general(a, b, (((0,), (0,)), ((), ())), preferred_element_type=f32)


def lhs_of(s):
    return jnp.concatenate(s, axis=1)


def rhs_of(s):
    y = jnp.concatenate(s, axis=1)
    return jnp.concatenate([y, y], axis=0)


def mm(a, b):
    o = dot(lhs_of(a), rhs_of(b))
    return o[:, :F] + o[:, F:]


def mm_all(pairs):
    return [mm(a, b) for a, b in pairs]


def map_product(p, r):
    ph, pl_ = split(p)
    rh, rl = split(r)
    return dot(jnp.concatenate([ph, pl_], axis=1), jnp.concatenate([rh, rh], axis=0)) + dot(ph, rl)


HB = 4


def half_of(mine, w):
    return w[2] if mine else 1 - w[2]


def local_kernel(mine, w_ref, k_ref, v_ref, b_ref, map_ref, xh_ref, xl_ref, r_ref):
    g = pl.program_id(0)
    first_head = half_of(mine, w_ref) * 4 + g * HB
    beta_rows = b_ref[...]
    beta_cols = jnp.transpose(jnp.concatenate([beta_rows, jnp.zeros((F - HEADS, TOK), f32)], axis=0))
    lane = lax.broadcasted_iota(jnp.int32, (TOK, F), 1)
    row = lax.broadcasted_iota(jnp.int32, (F, F), 0)
    col = lax.broadcasted_iota(jnp.int32, (F, F), 1)
    eye = (row == col).astype(f32)
    strict = row > col
    in16 = jnp.logical_and(strict, (row // 16) == (col // 16))
    in64 = jnp.logical_and((row // 64) == (col // 64), (row // 16) > (col // 16))
    in128 = (row // 64) > (col // 64)

    stat = jnp.zeros((TOK, F), f32)
    ks, rs, bs, kraw = [], [], [], []
    for i in range(HB):
        k = k_ref[:, i * F:(i + 1) * F]
        kf = k.astype(f32)
        r = lax.rsqrt(jnp.sum(kf * kf, axis=-1, keepdims=True) + EPS)
        kf = jnp.where(r > 0.0, kf, 0.0)
        b = jnp.sum(jnp.where(lane == first_head + i, beta_cols, 0.0), axis=-1, keepdims=True)
        ks.append(kf)
        kraw.append(kf.astype(bf16))
        rs.append(r)
        bs.append(b)
        stat = jnp.where(lane == 2 * i, r, stat)
        stat = jnp.where(lane == 2 * i + 1, b, stat)
    stat_t = jnp.transpose(stat)
    r_ref[g] = stat_t[0:8, :]

    tiles = []
    cross = []
    for i in range(HB):
        r_row = stat_t[2 * i:2 * i + 1, :]
        br = bs[i] * rs[i]
        k1, k2 = kraw[i][:F], kraw[i][F:]
        g11 = dot_nt(k1, k1)
        g2 = dot_nt(k2, kraw[i])
        a11 = g11 * br[:F] * r_row[:, :F]
        a2 = g2 * br[F:] * r_row
        tiles += [a11, a2[:, F:]]
        cross.append(a2[:, :F])
    n = [jnp.where(in16, a, 0.0) for a in tiles]
    ns = [split(a) for a in n]
    n2 = mm_all(zip(ns, ns))
    n2s = [split(a) for a in n2]
    n4 = mm_all(zip(n2s, n2s))
    q1 = mm_all(zip(ns, n2s))
    n4s = [split(a) for a in n4]
    r1 = [eye - a + b - c for a, b, c in zip(n, n2, q1)]
    n8 = mm_all(zip(n4s, n4s))
    q2 = mm_all(zip([split(a) for a in r1], n4s))
    r2 = [a + b for a, b in zip(r1, q2)]
    q3 = mm_all(zip([split(a) for a in r2], [split(a) for a in n8]))
    d = [a + b for a, b in zip(r2, q3)]
    ds = [split(a) for a in d]
    m = mm_all(zip(ds, [split(jnp.where(in64, a, 0.0)) for a in tiles]))
    ms = [split(a) for a in m]
    m2 = mm_all(zip(ms, ms))
    e = [a + b for a, b in zip(d, mm_all(zip([split(a) for a in m2], ds)))]
    t = [a - b for a, b in zip(e, mm_all(zip(ms, [split(a) for a in e])))]
    ts = [split(a) for a in t]
    u = mm_all(zip([split(jnp.where(in128, a, 0.0)) for a in tiles], ts))
    t = [a - b for a, b in zip(t, mm_all(zip(ts, [split(a) for a in u])))]
    ts = [split(a) for a in t]
    c1 = mm_all(zip([split(a) for a in cross], ts[0::2]))
    t21 = [-a for a in mm_all(zip(ts[1::2], [split(a) for a in c1]))]

    for i in range(HB):
        b_row = stat_t[2 * i + 1:2 * i + 2, :]
        t11h, t11l = split(t[2 * i] * b_row[:, :F])
        t2h, t2l = split(jnp.concatenate([t21[i], t[2 * i + 1]], axis=1) * b_row)
        kn = ks[i] * rs[i]
        knh, knl = split(kn)
        v = v_ref[:, i * F:(i + 1) * F]
        bh = jnp.concatenate([knh, v], axis=1)
        bh1 = bh[:F]
        x1 = dot(jnp.concatenate([t11h, t11l], axis=1), jnp.concatenate([bh1, bh1], axis=0))
        x2 = dot(t2h, bh) + dot(t2l, bh)
        y1 = dot(t11h, knl[:F])
        y2 = dot(t2h, knl)
        x = jnp.concatenate([x1, x2], axis=0)
        y = jnp.concatenate([y1, y2], axis=0)
        x = jnp.concatenate([x[:, :F] + y, x[:, F:]], axis=1)
        xh, xl = split(x)
        xh_ref[g * HB + i] = xh
        xl_ref[g * HB + i] = xl
        zh, zl = split(x * rs[i])
        pw = dot_tn(kraw[i], zh) + dot_tn(kraw[i], zl)
        map_ref[g * HB + i] = jnp.concatenate([eye - pw[:, :F], pw[:, F:]], axis=1)


def vmem(shape, dtype=f32):
    return pltpu.VMEM(shape, dtype)


PARAMS = pltpu.CompilerParams(vmem_limit_bytes=24 << 20)


def in_hbm(x):
    return pltpu.with_memory_space_constraint(x, pltpu.HBM)


def in_vmem(x):
    return pltpu.with_memory_space_constraint(x, pltpu.VMEM)


ANYV = pl.BlockSpec(memory_space=pltpu.VMEM)


def local_maps(mine, where, k, v, beta_rows):
    steps = 4 // HB
    cols = pl.BlockSpec((TOK, HB * F), lambda g, w: (0, half_of(mine, w) * steps + g))
    return pl.pallas_call(
        functools.partial(local_kernel, mine),
        grid_spec=pltpu.PrefetchScalarGridSpec(
            num_scalar_prefetch=1,
            grid=(steps,),
            in_specs=[cols, cols, pl.BlockSpec((HEADS, TOK), lambda g, w: (0, 0))],
            out_specs=[ANYV] * 4,
        ),
        out_shape=[
            vmem((4, F, 2 * F)),
            vmem((4, TOK, 2 * F), bf16),
            vmem((4, TOK, 2 * F), bf16),
            vmem((steps, 8, TOK)),
        ],
        compiler_params=PARAMS,
        name="local_maps",
    )(where, in_hbm(k), in_hbm(v), in_hbm(beta_rows))


def reads_kernel(w_ref, q_ref, k_ref, xh_ref, xl_ref, r_ref, m_ref, qh_ref, ql_ref, y_ref):
    g = pl.program_id(0)
    row = lax.broadcasted_iota(jnp.int32, (TOK, TOK), 0)
    col = lax.broadcasted_iota(jnp.int32, (TOK, TOK), 1)
    causal = row >= col
    for i in range(HB):
        q = q_ref[:, i * F:(i + 1) * F]
        k = k_ref[:, i * F:(i + 1) * F]
        r_row = r_ref[g, 2 * i:2 * i + 1, :]
        s = dot_nt(q, k) * r_row
        s = jnp.where(jnp.logical_and(causal, r_row > 0.0), s, 0.0)
        sh, sl = split(s)
        n = g * HB + i
        xh, xl = xh_ref[n], xl_ref[n]
        o = dot(sh, xh) + (dot(sl, xh) + dot(sh, xl))
        qe = q.astype(f32) - o[:, :F]
        qh, ql = split(qe)
        qh_ref[n] = qh
        ql_ref[n] = ql
        y_ref[n] = o[:, F:]

        @pl.when(w_ref[2] == 1)
        def _():
            z = map_product(qe, m_ref[n])
            zh, zl = split(z[:, :F])
            qh_ref[n] = zh
            ql_ref[n] = zl
            y_ref[n] = o[:, F:] + z[:, F:]


def local_reads(mine, where, q, k, xh, xl, r, first):
    steps = 4 // HB
    cols = pl.BlockSpec((TOK, HB * F), lambda g, w: (0, half_of(mine, w) * steps + g))
    return pl.pallas_call(
        reads_kernel,
        grid_spec=pltpu.PrefetchScalarGridSpec(
            num_scalar_prefetch=1,
            grid=(steps,),
            in_specs=[cols, cols] + [ANYV] * 4,
            out_specs=[ANYV] * 3,
        ),
        out_shape=[vmem((4, TOK, F), bf16), vmem((4, TOK, F), bf16), vmem((4, TOK, F))],
        compiler_params=PARAMS,
        name="local_reads",
    )(where, in_hbm(q), in_hbm(k), *[in_vmem(a) for a in (xh, xl, r, first)])


def after(p_then, m):
    o = map_product(p_then[:, :F], m)
    return jnp.concatenate([o[:, :F], o[:, F:] + p_then[:, F:]], axis=1)


def stage(kernel, where, outs, *args, scratch=()):
    return pl.pallas_call(
        kernel,
        in_specs=[pl.BlockSpec(memory_space=pltpu.SMEM)] + [ANYV] * len(args),
        out_specs=[ANYV] * len(outs),
        out_shape=list(outs),
        scratch_shapes=list(scratch),
        compiler_params=PARAMS,
    )(where, *[in_vmem(a) for a in args])


def pair_kernel(w_ref, own_ref, got_ref, *out_refs):
    z, c = w_ref[1], w_ref[2]
    for k in range(4):
        j = lax.rem(z + k, 4)
        own = own_ref[j]
        got = got_ref[j]
        out_refs[k][...] = after(jnp.where(c == 0, got, own), jnp.where(c == 0, own, got))


def chain_kernel(w_ref, m0_ref, m1_ref, m2_ref, m3_ref, pre_ref, all_ref, maps_ref):
    z = w_ref[1]
    for k, ref in enumerate((m0_ref, m1_ref, m2_ref, m3_ref)):
        maps_ref[lax.rem(z - k + 4, 4)] = ref[...]
    m = maps_ref[0]
    pre_ref[0] = m
    for j in range(1, 4):
        m = after(maps_ref[j], m)
        if j < 3:
            pre_ref[j] = m
    all_ref[...] = m


def apply_map(m, s):
    return mm(split(m[:, :F]), split(s)) + m[:, F:]


def plane_kernel(w_ref, m3_ref, m2_ref, m1_ref, pre_ref, *out_refs):
    y, z = w_ref[0], w_ref[1]
    s = jnp.where(y >= 3, m3_ref[:, F:], 0.0)
    s = jnp.where(y >= 2, apply_map(m2_ref[...], s), 0.0)
    s = jnp.where(y >= 1, apply_map(m1_ref[...], s), 0.0)
    for k in range(4):
        j = lax.rem(z + k, 4)
        t = apply_map(pre_ref[jnp.maximum(j - 1, 0)], s)
        out_refs[k][...] = jnp.where(j == 0, s, t)


def order_kernel(w_ref, s0_ref, s1_ref, s2_ref, s3_ref, out_ref):
    z = w_ref[1]
    for k, ref in enumerate((s0_ref, s1_ref, s2_ref, s3_ref)):
        out_ref[lax.rem(z - k + 4, 4)] = ref[...]


def out_kernel(w_ref, qh_ref, ql_ref, y_ref, s_ref, g_ref, o_ref):
    mixed = [mm((qh_ref[i], ql_ref[i]), split(s_ref[i])) + y_ref[i] for i in range(4)]
    for i, m in enumerate(mixed):
        ms = jnp.mean(m * m, axis=-1, keepdims=True)
        o_ref[:, i * F:(i + 1) * F] = (m * lax.rsqrt(ms + EPS) * g_ref[...]).astype(bf16)


def outputs(where, qh, ql, y, s, gain):
    return stage(out_kernel, where, [vmem((TOK, 4 * F), bf16)], qh, ql, y, s, gain)[0]


def shift(x, axis, k):
    return lax.ppermute(x, axis, [(i, (i + k) % 4) for i in range(4)])


def swap(x, axis, k):
    n = 2 if axis == "core" else 4
    return lax.ppermute(x, axis, [(i, i ^ k) for i in range(n)])


def body(query_rows, key_rows, value_rows, beta, norm_gain, out_cotangent):
    yi, zi, ci, hi = (lax.axis_index(a).astype(jnp.int32) for a in ("y", "z", "core", "head"))
    where = jnp.stack([yi, zi, ci, hi])

    cot = lax.ppermute(out_cotangent, ("y", "head"), [(a * 4 + b, b * 4 + a) for a in range(4) for b in range(4)])
    cot2 = jnp.stack([cot, swap(cot, "head", 1)])
    cots = jnp.concatenate([cot2, swap(cot2, "head", 3)])
    gain = norm_gain.reshape(1, F)
    beta_rows = beta.T
    m_a, xh_a, xl_a, r_a = local_maps(False, where, key_rows, value_rows, beta_rows)
    got_b = swap(m_a, "core", 1)
    m_b, xh_b, xl_b, r_b = local_maps(True, where, key_rows, value_rows, beta_rows)
    got_a = swap(m_b, "core", 1)
    m4 = vmem((F, 2 * F))
    comb = stage(pair_kernel, where, [m4] * 4, m_b, got_b)
    got = [comb[0]]
    for k in (1, 2, 3):
        got.append(shift(comb[k], "z", k))
    rd_b = local_reads(True, where, query_rows, key_rows, xh_b, xl_b, r_b, got_b)
    rd_a = local_reads(False, where, query_rows, key_rows, xh_a, xl_a, r_a, got_a)
    pre, total = stage(chain_kernel, where, [vmem((3, F, 2 * F)), m4], *got, scratch=[pltpu.VMEM((4, F, 2 * F), f32)])
    planes = []
    for k in (3, 2, 1):
        planes.append(shift(total, "y", k))
    sc = stage(plane_kernel, where, [vmem((F, F))] * 4, *planes, pre)
    sx = [sc[0]]
    for k in (1, 2, 3):
        sx.append(shift(sc[k], "z", k))
    s_b, = stage(order_kernel, where, [vmem((4, F, F))], *sx)
    s_a = swap(s_b, "core", 1)
    att_b = outputs(where, *rd_b, s_b, gain)
    up_b = shift(att_b, "y", 1)
    dn_b = shift(att_b, "y", -1)
    att_a = outputs(where, *rd_a, s_a, gain)
    up_a = shift(att_a, "y", 1)
    dn_a = shift(att_a, "y", -1)
    far_b = shift(up_b, "y", 1)
    far_a = shift(dn_a, "y", -1)

    parts = stage(part_kernel, where, [vmem((4 * F, 8 * F))] * 2, cots, att_b, att_a, up_b, up_a, dn_b, dn_a)
    w_send, = stage(functools.partial(last_kernel, 0), where, [vmem((4 * F, 8 * F), bf16)], cots, far_b, far_a, parts[0])
    w_got = swap(w_send, "core", 1)
    w, = stage(functools.partial(last_kernel, 1), where, [vmem((4 * F, 8 * F))], cots, far_b, far_a, parts[1])
    quarter = vmem((2 * F, 4 * F), bf16)
    kept = vmem((2 * F, 4 * F))
    on_b, on_a, k_b, k_a = stage(sum_kernel, where, [quarter, quarter, kept, kept], w, w_got)
    r_b = swap(on_b, "z", 1)
    r_a = swap(on_a, "z", 3)
    h_b = (k_b[F:] + r_b[F:].astype(f32)).astype(bf16)
    e_b = swap(h_b, "z", 3)
    h_a = (k_a[F:] + r_a[F:].astype(f32)).astype(bf16)
    e_a = swap(h_a, "z", 1)
    g_b = k_b[:F] + r_b[:F].astype(f32) + e_b.astype(f32)
    g_a = k_a[:F] + r_a[:F].astype(f32) + e_a.astype(f32)
    grad = jnp.where(ci == 0, jnp.concatenate([g_b, g_a], axis=1), jnp.concatenate([g_a, g_b], axis=1))
    attended = jnp.where(ci == 0, jnp.concatenate([att_b, att_a], axis=1), jnp.concatenate([att_a, att_b], axis=1))
    return attended, grad


def cot_rows(w_ref, cot_ref, k, part):
    d = lax.rem(w_ref[0] - k + 4, 4) ^ w_ref[3]
    j = d ^ (d >> 1)
    core = half_of(part == 1, w_ref)
    return jnp.concatenate(
        [cot_ref[j, :, pl.ds(pl.multiple_of((2 * n + core) * F, F), F)] for n in range(4)], axis=1
    )


def part_kernel(w_ref, cot_ref, *refs):
    for s in range(2):
        rows = jnp.concatenate([cot_rows(w_ref, cot_ref, k, s) for k in (0, 1, 3)], axis=0)
        for n in range(2):
            tall = jnp.concatenate([refs[n][...], refs[2 + n][...], refs[4 + n][...]], axis=0)
            refs[6 + s][:, n * 4 * F:(n + 1) * 4 * F] = dot_tn(rows, tall)


def last_kernel(s, w_ref, cot_ref, b_ref, a_ref, part_ref, out_ref):
    rows = cot_rows(w_ref, cot_ref, 2, s)
    for n, ref in enumerate((b_ref, a_ref)):
        cols = slice(n * 4 * F, (n + 1) * 4 * F)
        out_ref[:, cols] = (part_ref[:, cols] + dot_tn(rows, ref[...])).astype(out_ref.dtype)


def sum_kernel(w_ref, keep_ref, got_ref, on_b_ref, on_a_ref, k_b_ref, k_a_ref):
    z = w_ref[1]
    h = 4 * F
    for n, (on_ref, k_ref, first, second) in enumerate(((on_b_ref, k_b_ref, 1, 3), (on_a_ref, k_a_ref, 3, 1))):
        mine = slice(n * h, (n + 1) * h)
        theirs = slice((1 - n) * h, (2 - n) * h)
        for i, (ref, blk) in enumerate(((on_ref, z ^ first), (on_ref, z ^ 2), (k_ref, z), (k_ref, z ^ second))):
            rows = pl.ds(pl.multiple_of(blk * F, F), F)
            total = keep_ref[rows, mine] + got_ref[rows, theirs].astype(f32)
            ref[(i % 2) * F:(i % 2 + 1) * F, :] = total.astype(ref.dtype)


def solution(mesh):
    fine = Mesh(mesh.devices.reshape(4, 4, 2, 4), ("y", "z", "core", "head"))
    spec = P(("y", "z", "core"), "head")
    return jax.shard_map(
        body,
        mesh=fine,
        in_specs=(spec, spec, spec, spec, P(), spec),
        out_specs=(spec, spec),
        check_vma=False,
    )
```

```python
import functools

import jax
import jax.numpy as jnp
from jax import lax
from jax.experimental import pallas as pl
from jax.experimental.pallas import tpu as pltpu
from jax.sharding import Mesh, PartitionSpec as P


F = 128
TOK = 256
HEADS = 8
EPS = 1e-06
f32 = jnp.float32
bf16 = jnp.bfloat16
f16 = jnp.float16


def split(x):
    h = x.astype(bf16)
    return h, (x - h.astype(f32)).astype(bf16)


def dot(a, b):
    return jnp.dot(a, b, preferred_element_type=f32)


def dot_nt(a, b):
    return lax.dot_general(a, b, (((1,), (1,)), ((), ())), preferred_element_type=f32)


def dot_tn(a, b):
    return lax.dot_general(a, b, (((0,), (0,)), ((), ())), preferred_element_type=f32)


def lhs_of(s):
    return jnp.concatenate(s, axis=1)


def rhs_of(s):
    y = jnp.concatenate(s, axis=1)
    return jnp.concatenate([y, y], axis=0)


def mm(a, b):
    o = dot(lhs_of(a), rhs_of(b))
    return o[:, :F] + o[:, F:]


def mm_all(pairs):
    return [mm(a, b) for a, b in pairs]


def map_product(p, r):
    ph, pl_ = split(p)
    rh, rl = split(r)
    return dot(jnp.concatenate([ph, pl_], axis=1), jnp.concatenate([rh, rh], axis=0)) + dot(ph, rl)


HB = 4


def half_of(mine, w):
    return w[2] if mine else 1 - w[2]


def local_kernel(mine, w_ref, k_ref, v_ref, b_ref, map_ref, xh_ref, xl_ref, r_ref):
    g = pl.program_id(0)
    first_head = half_of(mine, w_ref) * 4 + g * HB
    beta_rows = b_ref[...]
    beta_cols = jnp.transpose(jnp.concatenate([beta_rows, jnp.zeros((F - HEADS, TOK), f32)], axis=0))
    lane = lax.broadcasted_iota(jnp.int32, (TOK, F), 1)
    row = lax.broadcasted_iota(jnp.int32, (F, F), 0)
    col = lax.broadcasted_iota(jnp.int32, (F, F), 1)
    eye = (row == col).astype(f32)
    strict = row > col
    in16 = jnp.logical_and(strict, (row // 16) == (col // 16))
    in64 = jnp.logical_and((row // 64) == (col // 64), (row // 16) > (col // 16))
    in128 = (row // 64) > (col // 64)

    stat = jnp.zeros((TOK, F), f32)
    ks, rs, bs, kraw = [], [], [], []
    for i in range(HB):
        k = k_ref[:, i * F:(i + 1) * F]
        kf = k.astype(f32)
        r = lax.rsqrt(jnp.sum(kf * kf, axis=-1, keepdims=True) + EPS)
        kf = jnp.where(r > 0.0, kf, 0.0)
        b = jnp.sum(jnp.where(lane == first_head + i, beta_cols, 0.0), axis=-1, keepdims=True)
        ks.append(kf)
        kraw.append(kf.astype(bf16))
        rs.append(r)
        bs.append(b)
        stat = jnp.where(lane == 2 * i, r, stat)
        stat = jnp.where(lane == 2 * i + 1, b, stat)
    stat_t = jnp.transpose(stat)
    r_ref[g] = stat_t[0:8, :]

    tiles = []
    cross = []
    for i in range(HB):
        r_row = stat_t[2 * i:2 * i + 1, :]
        br = bs[i] * rs[i]
        k1, k2 = kraw[i][:F], kraw[i][F:]
        g11 = dot_nt(k1, k1)
        g2 = dot_nt(k2, kraw[i])
        a11 = g11 * br[:F] * r_row[:, :F]
        a2 = g2 * br[F:] * r_row
        tiles += [a11, a2[:, F:]]
        cross.append(a2[:, :F])
    n = [jnp.where(in16, a, 0.0) for a in tiles]
    ns = [split(a) for a in n]
    n2 = mm_all(zip(ns, ns))
    n2s = [split(a) for a in n2]
    n4 = mm_all(zip(n2s, n2s))
    q1 = mm_all(zip(ns, n2s))
    n4s = [split(a) for a in n4]
    r1 = [eye - a + b - c for a, b, c in zip(n, n2, q1)]
    n8 = mm_all(zip(n4s, n4s))
    q2 = mm_all(zip([split(a) for a in r1], n4s))
    r2 = [a + b for a, b in zip(r1, q2)]
    q3 = mm_all(zip([split(a) for a in r2], [split(a) for a in n8]))
    d = [a + b for a, b in zip(r2, q3)]
    ds = [split(a) for a in d]
    m = mm_all(zip(ds, [split(jnp.where(in64, a, 0.0)) for a in tiles]))
    ms = [split(a) for a in m]
    m2 = mm_all(zip(ms, ms))
    e = [a + b for a, b in zip(d, mm_all(zip([split(a) for a in m2], ds)))]
    t = [a - b for a, b in zip(e, mm_all(zip(ms, [split(a) for a in e])))]
    ts = [split(a) for a in t]
    u = mm_all(zip([split(jnp.where(in128, a, 0.0)) for a in tiles], ts))
    t = [a - b for a, b in zip(t, mm_all(zip(ts, [split(a) for a in u])))]
    ts = [split(a) for a in t]
    c1 = mm_all(zip([split(a) for a in cross], ts[0::2]))
    t21 = [-a for a in mm_all(zip(ts[1::2], [split(a) for a in c1]))]

    for i in range(HB):
        b_row = stat_t[2 * i + 1:2 * i + 2, :]
        t11h, t11l = split(t[2 * i] * b_row[:, :F])
        t2h, t2l = split(jnp.concatenate([t21[i], t[2 * i + 1]], axis=1) * b_row)
        kn = ks[i] * rs[i]
        knh, knl = split(kn)
        v = v_ref[:, i * F:(i + 1) * F]
        bh = jnp.concatenate([knh, v], axis=1)
        bh1 = bh[:F]
        x1 = dot(jnp.concatenate([t11h, t11l], axis=1), jnp.concatenate([bh1, bh1], axis=0))
        x2 = dot(t2h, bh) + dot(t2l, bh)
        y1 = dot(t11h, knl[:F])
        y2 = dot(t2h, knl)
        x = jnp.concatenate([x1, x2], axis=0)
        y = jnp.concatenate([y1, y2], axis=0)
        x = jnp.concatenate([x[:, :F] + y, x[:, F:]], axis=1)
        xh, xl = split(x)
        xh_ref[g * HB + i] = xh
        xl_ref[g * HB + i] = xl
        zh, zl = split(x * rs[i])
        pw = dot_tn(kraw[i], zh) + dot_tn(kraw[i], zl)
        map_ref[g * HB + i] = jnp.concatenate([eye - pw[:, :F], pw[:, F:]], axis=1)


def vmem(shape, dtype=f32):
    return pltpu.VMEM(shape, dtype)


PARAMS = pltpu.CompilerParams(vmem_limit_bytes=24 << 20)


def in_hbm(x):
    return pltpu.with_memory_space_constraint(x, pltpu.HBM)


def in_vmem(x):
    return pltpu.with_memory_space_constraint(x, pltpu.VMEM)


ANYV = pl.BlockSpec(memory_space=pltpu.VMEM)


def local_maps(mine, where, k, v, beta_rows):
    steps = 4 // HB
    cols = pl.BlockSpec((TOK, HB * F), lambda g, w: (0, half_of(mine, w) * steps + g))
    return pl.pallas_call(
        functools.partial(local_kernel, mine),
        grid_spec=pltpu.PrefetchScalarGridSpec(
            num_scalar_prefetch=1,
            grid=(steps,),
            in_specs=[cols, cols, pl.BlockSpec((HEADS, TOK), lambda g, w: (0, 0))],
            out_specs=[ANYV] * 4,
        ),
        out_shape=[
            vmem((4, F, 2 * F)),
            vmem((4, TOK, 2 * F), bf16),
            vmem((4, TOK, 2 * F), bf16),
            vmem((steps, 8, TOK)),
        ],
        compiler_params=PARAMS,
        name="local_maps",
    )(where, in_hbm(k), in_hbm(v), in_hbm(beta_rows))


def reads_kernel(w_ref, q_ref, k_ref, xh_ref, xl_ref, r_ref, m_ref, qh_ref, ql_ref, y_ref):
    g = pl.program_id(0)
    row = lax.broadcasted_iota(jnp.int32, (TOK, TOK), 0)
    col = lax.broadcasted_iota(jnp.int32, (TOK, TOK), 1)
    causal = row >= col
    for i in range(HB):
        q = q_ref[:, i * F:(i + 1) * F]
        k = k_ref[:, i * F:(i + 1) * F]
        r_row = r_ref[g, 2 * i:2 * i + 1, :]
        s = dot_nt(q, k) * r_row
        s = jnp.where(jnp.logical_and(causal, r_row > 0.0), s, 0.0)
        sh, sl = split(s)
        n = g * HB + i
        xh, xl = xh_ref[n], xl_ref[n]
        o = dot(sh, xh) + (dot(sl, xh) + dot(sh, xl))
        qe = q.astype(f32) - o[:, :F]
        qh, ql = split(qe)
        qh_ref[n] = qh
        ql_ref[n] = ql
        y_ref[n] = o[:, F:]

        @pl.when(w_ref[2] == 1)
        def _():
            z = map_product(qe, m_ref[n])
            zh, zl = split(z[:, :F])
            qh_ref[n] = zh
            ql_ref[n] = zl
            y_ref[n] = o[:, F:] + z[:, F:]


def local_reads(mine, where, q, k, xh, xl, r, first):
    steps = 4 // HB
    cols = pl.BlockSpec((TOK, HB * F), lambda g, w: (0, half_of(mine, w) * steps + g))
    return pl.pallas_call(
        reads_kernel,
        grid_spec=pltpu.PrefetchScalarGridSpec(
            num_scalar_prefetch=1,
            grid=(steps,),
            in_specs=[cols, cols] + [ANYV] * 4,
            out_specs=[ANYV] * 3,
        ),
        out_shape=[vmem((4, TOK, F), bf16), vmem((4, TOK, F), bf16), vmem((4, TOK, F))],
        compiler_params=PARAMS,
        name="local_reads",
    )(where, in_hbm(q), in_hbm(k), *[in_vmem(a) for a in (xh, xl, r, first)])


def after(p_then, m):
    o = map_product(p_then[:, :F], m)
    return jnp.concatenate([o[:, :F], o[:, F:] + p_then[:, F:]], axis=1)


SHRINK = 1.0 / 32.0


def packed(m):
    return jnp.concatenate([m[:, :F], m[:, F:] * SHRINK], axis=1)


def unpacked(m):
    return jnp.concatenate([m[:, :F], m[:, F:] * (1.0 / SHRINK)], axis=1)


def stage(kernel, where, outs, *args, scratch=()):
    return pl.pallas_call(
        kernel,
        in_specs=[pl.BlockSpec(memory_space=pltpu.SMEM)] + [ANYV] * len(args),
        out_specs=[ANYV] * len(outs),
        out_shape=list(outs),
        scratch_shapes=list(scratch),
        compiler_params=PARAMS,
    )(where, *[in_vmem(a) for a in args])


def pair_kernel(w_ref, own_ref, got_ref, *out_refs):
    z, c = w_ref[1], w_ref[2]
    for k in range(4):
        j = lax.rem(z + k, 4)
        own = own_ref[j]
        got = got_ref[j]
        m = after(jnp.where(c == 0, got, own), jnp.where(c == 0, own, got))
        out_refs[k][...] = m if k == 0 else packed(m)


def chain_kernel(w_ref, m0_ref, m1_ref, m2_ref, m3_ref, pre_ref, all_ref, maps_ref):
    z = w_ref[1]
    for k, ref in enumerate((m0_ref, m1_ref, m2_ref, m3_ref)):
        maps_ref[lax.rem(z - k + 4, 4)] = ref[...] if k == 0 else unpacked(ref[...])
    m = maps_ref[0]
    pre_ref[0] = m
    for j in range(1, 4):
        m = after(maps_ref[j], m)
        if j < 3:
            pre_ref[j] = m
    all_ref[...] = packed(m)


def apply_map(m, s):
    return mm(split(m[:, :F]), split(s)) + m[:, F:]


def plane_kernel(w_ref, m3_ref, m2_ref, m1_ref, pre_ref, *out_refs):
    y, z = w_ref[0], w_ref[1]
    s = jnp.where(y >= 3, unpacked(m3_ref[...])[:, F:], 0.0)
    s = jnp.where(y >= 2, apply_map(unpacked(m2_ref[...]), s), 0.0)
    s = jnp.where(y >= 1, apply_map(unpacked(m1_ref[...]), s), 0.0)
    for k in range(4):
        j = lax.rem(z + k, 4)
        t = apply_map(pre_ref[jnp.maximum(j - 1, 0)], s)
        out_refs[k][...] = jnp.where(j == 0, s, t)


def order_kernel(w_ref, s0_ref, s1_ref, s2_ref, s3_ref, out_ref):
    z = w_ref[1]
    for k, ref in enumerate((s0_ref, s1_ref, s2_ref, s3_ref)):
        out_ref[lax.rem(z - k + 4, 4)] = ref[...]


def out_kernel(w_ref, qh_ref, ql_ref, y_ref, s_ref, g_ref, o_ref):
    mixed = [mm((qh_ref[i], ql_ref[i]), split(s_ref[i])) + y_ref[i] for i in range(4)]
    for i, m in enumerate(mixed):
        ms = jnp.mean(m * m, axis=-1, keepdims=True)
        o_ref[:, i * F:(i + 1) * F] = (m * lax.rsqrt(ms + EPS) * g_ref[...]).astype(bf16)


def outputs(where, qh, ql, y, s, gain):
    return stage(out_kernel, where, [vmem((TOK, 4 * F), bf16)], qh, ql, y, s, gain)[0]


def shift(x, axis, k):
    return lax.ppermute(x, axis, [(i, (i + k) % 4) for i in range(4)])


def swap(x, axis, k):
    n = 2 if axis == "core" else 4
    return lax.ppermute(x, axis, [(i, i ^ k) for i in range(n)])


def body(query_rows, key_rows, value_rows, beta, norm_gain, out_cotangent):
    yi, zi, ci, hi = (lax.axis_index(a).astype(jnp.int32) for a in ("y", "z", "core", "head"))
    where = jnp.stack([yi, zi, ci, hi])

    cot = lax.ppermute(out_cotangent, ("y", "head"), [(a * 4 + b, b * 4 + a) for a in range(4) for b in range(4)])
    cot2 = jnp.stack([cot, swap(cot, "head", 1)])
    cots = jnp.concatenate([cot2, swap(cot2, "head", 3)])
    gain = norm_gain.reshape(1, F)
    beta_rows = beta.T
    m_a, xh_a, xl_a, r_a = local_maps(False, where, key_rows, value_rows, beta_rows)
    got_b = swap(m_a, "core", 1)
    m_b, xh_b, xl_b, r_b = local_maps(True, where, key_rows, value_rows, beta_rows)
    got_a = swap(m_b, "core", 1)
    m4 = vmem((F, 2 * F))
    comb = stage(pair_kernel, where, [m4] * 4, m_b, got_b)
    got = [comb[0]]
    for k in (1, 2, 3):
        got.append(shift(comb[k].astype(f16), "z", k).astype(f32))
    rd_b = local_reads(True, where, query_rows, key_rows, xh_b, xl_b, r_b, got_b)
    rd_a = local_reads(False, where, query_rows, key_rows, xh_a, xl_a, r_a, got_a)
    pre, total = stage(chain_kernel, where, [vmem((3, F, 2 * F)), m4], *got, scratch=[pltpu.VMEM((4, F, 2 * F), f32)])
    planes = []
    for k in (3, 2, 1):
        planes.append(shift(total.astype(f16), "y", k).astype(f32))
    sc = stage(plane_kernel, where, [vmem((F, F))] * 4, *planes, pre)
    sx = [sc[0]]
    for k in (1, 2, 3):
        sx.append(shift(sc[k], "z", k))
    s_b, = stage(order_kernel, where, [vmem((4, F, F))], *sx)
    s_a = swap(s_b, "core", 1)
    att_b = outputs(where, *rd_b, s_b, gain)
    up_b = shift(att_b, "y", 1)
    dn_b = shift(att_b, "y", -1)
    att_a = outputs(where, *rd_a, s_a, gain)
    up_a = shift(att_a, "y", 1)
    dn_a = shift(att_a, "y", -1)
    far_b = shift(up_b, "y", 1)
    far_a = shift(dn_a, "y", -1)

    parts = stage(part_kernel, where, [vmem((4 * F, 8 * F))] * 2, cots, att_b, att_a, up_b, up_a, dn_b, dn_a)
    w_send, = stage(functools.partial(last_kernel, 0), where, [vmem((4 * F, 8 * F), bf16)], cots, far_b, far_a, parts[0])
    w_got = swap(w_send, "core", 1)
    w, = stage(functools.partial(last_kernel, 1), where, [vmem((4 * F, 8 * F))], cots, far_b, far_a, parts[1])
    quarter = vmem((2 * F, 4 * F), bf16)
    kept = vmem((2 * F, 4 * F))
    on_b, on_a, k_b, k_a = stage(sum_kernel, where, [quarter, quarter, kept, kept], w, w_got)
    r_b = swap(on_b, "z", 1)
    r_a = swap(on_a, "z", 3)
    h_b = (k_b[F:] + r_b[F:].astype(f32)).astype(bf16)
    e_b = swap(h_b, "z", 3)
    h_a = (k_a[F:] + r_a[F:].astype(f32)).astype(bf16)
    e_a = swap(h_a, "z", 1)
    g_b = k_b[:F] + r_b[:F].astype(f32) + e_b.astype(f32)
    g_a = k_a[:F] + r_a[:F].astype(f32) + e_a.astype(f32)
    grad = jnp.where(ci == 0, jnp.concatenate([g_b, g_a], axis=1), jnp.concatenate([g_a, g_b], axis=1))
    attended = jnp.where(ci == 0, jnp.concatenate([att_b, att_a], axis=1), jnp.concatenate([att_a, att_b], axis=1))
    return attended, grad


def cot_rows(w_ref, cot_ref, k, part):
    d = lax.rem(w_ref[0] - k + 4, 4) ^ w_ref[3]
    j = d ^ (d >> 1)
    core = half_of(part == 1, w_ref)
    return jnp.concatenate(
        [cot_ref[j, :, pl.ds(pl.multiple_of((2 * n + core) * F, F), F)] for n in range(4)], axis=1
    )


def part_kernel(w_ref, cot_ref, *refs):
    for s in range(2):
        rows = jnp.concatenate([cot_rows(w_ref, cot_ref, k, s) for k in (0, 1, 3)], axis=0)
        for n in range(2):
            tall = jnp.concatenate([refs[n][...], refs[2 + n][...], refs[4 + n][...]], axis=0)
            refs[6 + s][:, n * 4 * F:(n + 1) * 4 * F] = dot_tn(rows, tall)


def last_kernel(s, w_ref, cot_ref, b_ref, a_ref, part_ref, out_ref):
    rows = cot_rows(w_ref, cot_ref, 2, s)
    for n, ref in enumerate((b_ref, a_ref)):
        cols = slice(n * 4 * F, (n + 1) * 4 * F)
        out_ref[:, cols] = (part_ref[:, cols] + dot_tn(rows, ref[...])).astype(out_ref.dtype)


def sum_kernel(w_ref, keep_ref, got_ref, on_b_ref, on_a_ref, k_b_ref, k_a_ref):
    z = w_ref[1]
    h = 4 * F
    for n, (on_ref, k_ref, first, second) in enumerate(((on_b_ref, k_b_ref, 1, 3), (on_a_ref, k_a_ref, 3, 1))):
        mine = slice(n * h, (n + 1) * h)
        theirs = slice((1 - n) * h, (2 - n) * h)
        for i, (ref, blk) in enumerate(((on_ref, z ^ first), (on_ref, z ^ 2), (k_ref, z), (k_ref, z ^ second))):
            rows = pl.ds(pl.multiple_of(blk * F, F), F)
            total = keep_ref[rows, mine] + got_ref[rows, theirs].astype(f32)
            ref[(i % 2) * F:(i % 2 + 1) * F, :] = total.astype(ref.dtype)


def solution(mesh):
    fine = Mesh(mesh.devices.reshape(4, 4, 2, 4), ("y", "z", "core", "head"))
    spec = P(("y", "z", "core"), "head")
    return jax.shard_map(
        body,
        mesh=fine,
        in_specs=(spec, spec, spec, spec, P(), spec),
        out_specs=(spec, spec),
        check_vma=False,
    )
```

```python
import functools

import jax
import jax.numpy as jnp
from jax import lax
from jax.experimental import pallas as pl
from jax.experimental.pallas import tpu as pltpu
from jax.sharding import Mesh, PartitionSpec as P


F = 128
TOK = 256
HEADS = 8
EPS = 1e-06
f32 = jnp.float32
bf16 = jnp.bfloat16
f16 = jnp.float16


def split(x):
    h = x.astype(bf16)
    return h, (x - h.astype(f32)).astype(bf16)


def dot(a, b):
    return jnp.dot(a, b, preferred_element_type=f32)


def dot_nt(a, b):
    return lax.dot_general(a, b, (((1,), (1,)), ((), ())), preferred_element_type=f32)


def dot_tn(a, b):
    return lax.dot_general(a, b, (((0,), (0,)), ((), ())), preferred_element_type=f32)


def lhs_of(s):
    return jnp.concatenate(s, axis=1)


def rhs_of(s):
    y = jnp.concatenate(s, axis=1)
    return jnp.concatenate([y, y], axis=0)


def mm(a, b):
    o = dot(lhs_of(a), rhs_of(b))
    return o[:, :F] + o[:, F:]


def mm_two(a, c, b):
    o = dot(jnp.concatenate([lhs_of(a), lhs_of(c)], axis=0), rhs_of(b))
    o = o[:, :F] + o[:, F:]
    return o[:F], o[F:]


def mm_all(pairs):
    return [mm(a, b) for a, b in pairs]


def map_product(p, r):
    ph, pl_ = split(p)
    rh, rl = split(r)
    return dot(jnp.concatenate([ph, pl_], axis=1), jnp.concatenate([rh, rh], axis=0)) + dot(ph, rl)


HB = 4


def half_of(mine, w):
    return w[2] if mine else 1 - w[2]


def local_kernel(mine, w_ref, k_ref, v_ref, b_ref, map_ref, xh_ref, xl_ref, r_ref):
    g = pl.program_id(0)
    first_head = half_of(mine, w_ref) * 4 + g * HB
    beta_rows = b_ref[...]
    beta_cols = jnp.transpose(jnp.concatenate([beta_rows, jnp.zeros((F - HEADS, TOK), f32)], axis=0))
    lane = lax.broadcasted_iota(jnp.int32, (TOK, F), 1)
    row = lax.broadcasted_iota(jnp.int32, (F, F), 0)
    col = lax.broadcasted_iota(jnp.int32, (F, F), 1)
    eye = (row == col).astype(f32)
    strict = row > col
    in16 = jnp.logical_and(strict, (row // 16) == (col // 16))
    in64 = jnp.logical_and((row // 64) == (col // 64), (row // 16) > (col // 16))
    in128 = (row // 64) > (col // 64)

    stat = jnp.zeros((TOK, F), f32)
    ks, rs, bs, kraw = [], [], [], []
    for i in range(HB):
        k = k_ref[:, i * F:(i + 1) * F]
        kf = k.astype(f32)
        r = lax.rsqrt(jnp.sum(kf * kf, axis=-1, keepdims=True) + EPS)
        kf = jnp.where(r > 0.0, kf, 0.0)
        b = jnp.sum(jnp.where(lane == first_head + i, beta_cols, 0.0), axis=-1, keepdims=True)
        ks.append(kf)
        kraw.append(kf.astype(bf16))
        rs.append(r)
        bs.append(b)
        stat = jnp.where(lane == 2 * i, r, stat)
        stat = jnp.where(lane == 2 * i + 1, b, stat)
    stat_t = jnp.transpose(stat)
    r_ref[g] = stat_t[0:8, :]

    tiles = []
    cross = []
    for i in range(HB):
        r_row = stat_t[2 * i:2 * i + 1, :]
        br = bs[i] * rs[i]
        k1, k2 = kraw[i][:F], kraw[i][F:]
        g11 = dot_nt(k1, k1)
        g2 = dot_nt(k2, kraw[i])
        a11 = g11 * br[:F] * r_row[:, :F]
        a2 = g2 * br[F:] * r_row
        tiles += [a11, a2[:, F:]]
        cross.append(a2[:, :F])
    n = [jnp.where(in16, a, 0.0) for a in tiles]
    ns = [split(a) for a in n]
    n2 = mm_all(zip(ns, ns))
    n2s = [split(a) for a in n2]
    n4, q1 = zip(*[mm_two(b, a, b) for a, b in zip(ns, n2s)])
    n4s = [split(a) for a in n4]
    r1 = [eye - a + b - c for a, b, c in zip(n, n2, q1)]
    n8, q2 = zip(*[mm_two(b, split(a), b) for a, b in zip(r1, n4s)])
    r2 = [a + b for a, b in zip(r1, q2)]
    q3 = mm_all(zip([split(a) for a in r2], [split(a) for a in n8]))
    d = [a + b for a, b in zip(r2, q3)]
    ds = [split(a) for a in d]
    m = mm_all(zip(ds, [split(jnp.where(in64, a, 0.0)) for a in tiles]))
    ms = [split(a) for a in m]
    m2 = mm_all(zip(ms, ms))
    e = [a + b for a, b in zip(d, mm_all(zip([split(a) for a in m2], ds)))]
    t = [a - b for a, b in zip(e, mm_all(zip(ms, [split(a) for a in e])))]
    ts = [split(a) for a in t]
    u = mm_all(zip([split(jnp.where(in128, a, 0.0)) for a in tiles], ts))
    t = [a - b for a, b in zip(t, mm_all(zip(ts, [split(a) for a in u])))]
    ts = [split(a) for a in t]
    c1 = mm_all(zip([split(a) for a in cross], ts[0::2]))
    t21 = [-a for a in mm_all(zip(ts[1::2], [split(a) for a in c1]))]

    for i in range(HB):
        b_row = stat_t[2 * i + 1:2 * i + 2, :]
        t11h, t11l = split(t[2 * i] * b_row[:, :F])
        t2h, t2l = split(jnp.concatenate([t21[i], t[2 * i + 1]], axis=1) * b_row)
        kn = ks[i] * rs[i]
        knh, knl = split(kn)
        v = v_ref[:, i * F:(i + 1) * F]
        bh = jnp.concatenate([knh, v], axis=1)
        bh1 = bh[:F]
        x1 = dot(jnp.concatenate([t11h, t11l], axis=1), jnp.concatenate([bh1, bh1], axis=0))
        x2 = dot(t2h, bh) + dot(t2l, bh)
        y1 = dot(t11h, knl[:F])
        y2 = dot(t2h, knl)
        x = jnp.concatenate([x1, x2], axis=0)
        y = jnp.concatenate([y1, y2], axis=0)
        x = jnp.concatenate([x[:, :F] + y, x[:, F:]], axis=1)
        xh, xl = split(x)
        xh_ref[g * HB + i] = xh
        xl_ref[g * HB + i] = xl
        zh, zl = split(x * rs[i])
        pw = dot_tn(kraw[i], zh) + dot_tn(kraw[i], zl)
        map_ref[g * HB + i] = jnp.concatenate([eye - pw[:, :F], pw[:, F:]], axis=1)


def vmem(shape, dtype=f32):
    return pltpu.VMEM(shape, dtype)


PARAMS = pltpu.CompilerParams(vmem_limit_bytes=24 << 20)


def in_hbm(x):
    return pltpu.with_memory_space_constraint(x, pltpu.HBM)


def in_vmem(x):
    return pltpu.with_memory_space_constraint(x, pltpu.VMEM)


ANYV = pl.BlockSpec(memory_space=pltpu.VMEM)


def local_maps(mine, where, k, v, beta_rows):
    steps = 4 // HB
    cols = pl.BlockSpec((TOK, HB * F), lambda g, w: (0, half_of(mine, w) * steps + g))
    return pl.pallas_call(
        functools.partial(local_kernel, mine),
        grid_spec=pltpu.PrefetchScalarGridSpec(
            num_scalar_prefetch=1,
            grid=(steps,),
            in_specs=[cols, cols, pl.BlockSpec((HEADS, TOK), lambda g, w: (0, 0))],
            out_specs=[ANYV] * 4,
        ),
        out_shape=[
            vmem((4, F, 2 * F)),
            vmem((4, TOK, 2 * F), bf16),
            vmem((4, TOK, 2 * F), bf16),
            vmem((steps, 8, TOK)),
        ],
        compiler_params=PARAMS,
        name="local_maps",
    )(where, in_hbm(k), in_hbm(v), in_hbm(beta_rows))


def reads_kernel(w_ref, q_ref, k_ref, xh_ref, xl_ref, r_ref, m_ref, qh_ref, ql_ref, y_ref):
    g = pl.program_id(0)
    row = lax.broadcasted_iota(jnp.int32, (TOK, TOK), 0)
    col = lax.broadcasted_iota(jnp.int32, (TOK, TOK), 1)
    causal = row >= col
    for i in range(HB):
        q = q_ref[:, i * F:(i + 1) * F]
        k = k_ref[:, i * F:(i + 1) * F]
        r_row = r_ref[g, 2 * i:2 * i + 1, :]
        s = dot_nt(q, k) * r_row
        s = jnp.where(jnp.logical_and(causal, r_row > 0.0), s, 0.0)
        sh, sl = split(s)
        n = g * HB + i
        xh, xl = xh_ref[n], xl_ref[n]
        top = dot(jnp.concatenate([sh[:F, :F], sl[:F, :F]], axis=1), jnp.concatenate([xh[:F], xh[:F]], axis=0))
        top += dot(sh[:F, :F], xl[:F])
        o = jnp.concatenate([top, dot(sh[F:], xh) + (dot(sl[F:], xh) + dot(sh[F:], xl))], axis=0)
        qe = q.astype(f32) - o[:, :F]
        qh, ql = split(qe)
        qh_ref[n] = qh
        ql_ref[n] = ql
        y_ref[n] = o[:, F:]

        @pl.when(w_ref[2] == 1)
        def _():
            z = map_product(qe, m_ref[n])
            zh, zl = split(z[:, :F])
            qh_ref[n] = zh
            ql_ref[n] = zl
            y_ref[n] = o[:, F:] + z[:, F:]


def local_reads(mine, where, q, k, xh, xl, r, first):
    steps = 4 // HB
    cols = pl.BlockSpec((TOK, HB * F), lambda g, w: (0, half_of(mine, w) * steps + g))
    return pl.pallas_call(
        reads_kernel,
        grid_spec=pltpu.PrefetchScalarGridSpec(
            num_scalar_prefetch=1,
            grid=(steps,),
            in_specs=[cols, cols] + [ANYV] * 4,
            out_specs=[ANYV] * 3,
        ),
        out_shape=[vmem((4, TOK, F), bf16), vmem((4, TOK, F), bf16), vmem((4, TOK, F))],
        compiler_params=PARAMS,
        name="local_reads",
    )(where, in_hbm(q), in_hbm(k), *[in_vmem(a) for a in (xh, xl, r, first)])


def after(p_then, m):
    o = map_product(p_then[:, :F], m)
    return jnp.concatenate([o[:, :F], o[:, F:] + p_then[:, F:]], axis=1)


SHRINK = 1.0 / 32.0


def packed(m):
    return jnp.concatenate([m[:, :F], m[:, F:] * SHRINK], axis=1)


def unpacked(m):
    return jnp.concatenate([m[:, :F], m[:, F:] * (1.0 / SHRINK)], axis=1)


def stage(kernel, where, outs, *args, scratch=()):
    return pl.pallas_call(
        kernel,
        in_specs=[pl.BlockSpec(memory_space=pltpu.SMEM)] + [ANYV] * len(args),
        out_specs=[ANYV] * len(outs),
        out_shape=list(outs),
        scratch_shapes=list(scratch),
        compiler_params=PARAMS,
    )(where, *[in_vmem(a) for a in args])


def pair_kernel(w_ref, own_ref, got_ref, *out_refs):
    z, c = w_ref[1], w_ref[2]
    for k in range(4):
        j = lax.rem(z + k, 4)
        own = own_ref[j]
        got = got_ref[j]
        m = after(jnp.where(c == 0, got, own), jnp.where(c == 0, own, got))
        out_refs[k][...] = m if k == 0 else packed(m)


def chain_kernel(w_ref, m0_ref, m1_ref, m2_ref, m3_ref, pre_ref, all_ref, maps_ref):
    z = w_ref[1]
    for k, ref in enumerate((m0_ref, m1_ref, m2_ref, m3_ref)):
        maps_ref[lax.rem(z - k + 4, 4)] = ref[...] if k == 0 else unpacked(ref[...])
    m = maps_ref[0]
    pre_ref[0] = m
    for j in range(1, 4):
        m = after(maps_ref[j], m)
        if j < 3:
            pre_ref[j] = m
    all_ref[...] = packed(m)


def apply_map(m, s):
    return mm(split(m[:, :F]), split(s)) + m[:, F:]


def plane_kernel(w_ref, m3_ref, m2_ref, m1_ref, pre_ref, *out_refs):
    y, z = w_ref[0], w_ref[1]
    s = jnp.where(y >= 3, unpacked(m3_ref[...])[:, F:], 0.0)
    s = jnp.where(y >= 2, apply_map(unpacked(m2_ref[...]), s), 0.0)
    s = jnp.where(y >= 1, apply_map(unpacked(m1_ref[...]), s), 0.0)
    for k in range(4):
        j = lax.rem(z + k, 4)
        t = apply_map(pre_ref[jnp.maximum(j - 1, 0)], s)
        out_refs[k][...] = jnp.where(j == 0, s, t)


def order_kernel(w_ref, s0_ref, s1_ref, s2_ref, s3_ref, out_ref):
    z = w_ref[1]
    for k, ref in enumerate((s0_ref, s1_ref, s2_ref, s3_ref)):
        out_ref[lax.rem(z - k + 4, 4)] = ref[...]


def out_kernel(w_ref, qh_ref, ql_ref, y_ref, s_ref, g_ref, o_ref):
    mixed = [mm((qh_ref[i], ql_ref[i]), split(s_ref[i])) + y_ref[i] for i in range(4)]
    for i, m in enumerate(mixed):
        ms = jnp.mean(m * m, axis=-1, keepdims=True)
        o_ref[:, i * F:(i + 1) * F] = (m * lax.rsqrt(ms + EPS) * g_ref[...]).astype(bf16)


def outputs(where, qh, ql, y, s, gain):
    return stage(out_kernel, where, [vmem((TOK, 4 * F), bf16)], qh, ql, y, s, gain)[0]


def shift(x, axis, k):
    return lax.ppermute(x, axis, [(i, (i + k) % 4) for i in range(4)])


def swap(x, axis, k):
    n = 2 if axis == "core" else 4
    return lax.ppermute(x, axis, [(i, i ^ k) for i in range(n)])


def body(query_rows, key_rows, value_rows, beta, norm_gain, out_cotangent):
    yi, zi, ci, hi = (lax.axis_index(a).astype(jnp.int32) for a in ("y", "z", "core", "head"))
    where = jnp.stack([yi, zi, ci, hi])

    cot = lax.ppermute(out_cotangent, ("y", "head"), [(a * 4 + b, b * 4 + a) for a in range(4) for b in range(4)])
    cot2 = jnp.stack([cot, swap(cot, "head", 1)])
    cots = jnp.concatenate([cot2, swap(cot2, "head", 3)])
    gain = norm_gain.reshape(1, F)
    beta_rows = beta.T
    m_a, xh_a, xl_a, r_a = local_maps(False, where, key_rows, value_rows, beta_rows)
    got_b = swap(m_a, "core", 1)
    m_b, xh_b, xl_b, r_b = local_maps(True, where, key_rows, value_rows, beta_rows)
    got_a = swap(m_b, "core", 1)
    m4 = vmem((F, 2 * F))
    comb = stage(pair_kernel, where, [m4] * 4, m_b, got_b)
    got = [comb[0]]
    for k in (1, 2, 3):
        got.append(shift(comb[k].astype(f16), "z", k).astype(f32))
    rd_b = local_reads(True, where, query_rows, key_rows, xh_b, xl_b, r_b, got_b)
    rd_a = local_reads(False, where, query_rows, key_rows, xh_a, xl_a, r_a, got_a)
    pre, total = stage(chain_kernel, where, [vmem((3, F, 2 * F)), m4], *got, scratch=[pltpu.VMEM((4, F, 2 * F), f32)])
    planes = []
    for k in (3, 2, 1):
        planes.append(shift(total.astype(f16), "y", k).astype(f32))
    sc = stage(plane_kernel, where, [vmem((F, F))] * 4, *planes, pre)
    sx = [sc[0]]
    for k in (1, 2, 3):
        sx.append(shift(sc[k], "z", k))
    s_b, = stage(order_kernel, where, [vmem((4, F, F))], *sx)
    s_a = swap(s_b, "core", 1)
    att_b = outputs(where, *rd_b, s_b, gain)
    up_b = shift(att_b, "y", 1)
    dn_b = shift(att_b, "y", -1)
    att_a = outputs(where, *rd_a, s_a, gain)
    up_a = shift(att_a, "y", 1)
    dn_a = shift(att_a, "y", -1)
    far_b = shift(up_b, "y", 1)
    far_a = shift(dn_a, "y", -1)

    parts = stage(part_kernel, where, [vmem((4 * F, 8 * F))] * 2, cots, att_b, att_a, up_b, up_a, dn_b, dn_a)
    w_send, = stage(functools.partial(last_kernel, 0), where, [vmem((4 * F, 8 * F), bf16)], cots, far_b, far_a, parts[0])
    w_got = swap(w_send, "core", 1)
    w, = stage(functools.partial(last_kernel, 1), where, [vmem((4 * F, 8 * F))], cots, far_b, far_a, parts[1])
    quarter = vmem((2 * F, 4 * F), bf16)
    kept = vmem((2 * F, 4 * F))
    on_b, on_a, k_b, k_a = stage(sum_kernel, where, [quarter, quarter, kept, kept], w, w_got)
    r_b = swap(on_b, "z", 1)
    r_a = swap(on_a, "z", 3)
    h_b = (k_b[F:] + r_b[F:].astype(f32)).astype(bf16)
    e_b = swap(h_b, "z", 3)
    h_a = (k_a[F:] + r_a[F:].astype(f32)).astype(bf16)
    e_a = swap(h_a, "z", 1)
    g_b = k_b[:F] + r_b[:F].astype(f32) + e_b.astype(f32)
    g_a = k_a[:F] + r_a[:F].astype(f32) + e_a.astype(f32)
    grad = jnp.where(ci == 0, jnp.concatenate([g_b, g_a], axis=1), jnp.concatenate([g_a, g_b], axis=1))
    attended = jnp.where(ci == 0, jnp.concatenate([att_b, att_a], axis=1), jnp.concatenate([att_a, att_b], axis=1))
    return attended, grad


def cot_rows(w_ref, cot_ref, k, part):
    d = lax.rem(w_ref[0] - k + 4, 4) ^ w_ref[3]
    j = d ^ (d >> 1)
    core = half_of(part == 1, w_ref)
    return jnp.concatenate(
        [cot_ref[j, :, pl.ds(pl.multiple_of((2 * n + core) * F, F), F)] for n in range(4)], axis=1
    )


def part_kernel(w_ref, cot_ref, *refs):
    for s in range(2):
        rows = jnp.concatenate([cot_rows(w_ref, cot_ref, k, s) for k in (0, 1, 3)], axis=0)
        for n in range(2):
            tall = jnp.concatenate([refs[n][...], refs[2 + n][...], refs[4 + n][...]], axis=0)
            refs[6 + s][:, n * 4 * F:(n + 1) * 4 * F] = dot_tn(rows, tall)


def last_kernel(s, w_ref, cot_ref, b_ref, a_ref, part_ref, out_ref):
    rows = cot_rows(w_ref, cot_ref, 2, s)
    for n, ref in enumerate((b_ref, a_ref)):
        cols = slice(n * 4 * F, (n + 1) * 4 * F)
        out_ref[:, cols] = (part_ref[:, cols] + dot_tn(rows, ref[...])).astype(out_ref.dtype)


def sum_kernel(w_ref, keep_ref, got_ref, on_b_ref, on_a_ref, k_b_ref, k_a_ref):
    z = w_ref[1]
    h = 4 * F
    for n, (on_ref, k_ref, first, second) in enumerate(((on_b_ref, k_b_ref, 1, 3), (on_a_ref, k_a_ref, 3, 1))):
        mine = slice(n * h, (n + 1) * h)
        theirs = slice((1 - n) * h, (2 - n) * h)
        for i, (ref, blk) in enumerate(((on_ref, z ^ first), (on_ref, z ^ 2), (k_ref, z), (k_ref, z ^ second))):
            rows = pl.ds(pl.multiple_of(blk * F, F), F)
            total = keep_ref[rows, mine] + got_ref[rows, theirs].astype(f32)
            ref[(i % 2) * F:(i % 2 + 1) * F, :] = total.astype(ref.dtype)


def solution(mesh):
    fine = Mesh(mesh.devices.reshape(4, 4, 2, 4), ("y", "z", "core", "head"))
    spec = P(("y", "z", "core"), "head")
    return jax.shard_map(
        body,
        mesh=fine,
        in_specs=(spec, spec, spec, spec, P(), spec),
        out_specs=(spec, spec),
        check_vma=False,
    )
```

```python
import functools

import jax
import jax.numpy as jnp
from jax import lax
from jax.experimental import pallas as pl
from jax.experimental.pallas import tpu as pltpu
from jax.sharding import Mesh, PartitionSpec as P


F = 128
TOK = 256
HEADS = 8
EPS = 1e-06
f32 = jnp.float32
bf16 = jnp.bfloat16
f16 = jnp.float16


def split(x):
    h = x.astype(bf16)
    return h, (x - h.astype(f32)).astype(bf16)


def dot(a, b):
    return jnp.dot(a, b, preferred_element_type=f32)


def dot_nt(a, b):
    return lax.dot_general(a, b, (((1,), (1,)), ((), ())), preferred_element_type=f32)


def dot_tn(a, b):
    return lax.dot_general(a, b, (((0,), (0,)), ((), ())), preferred_element_type=f32)


def lhs_of(s):
    return jnp.concatenate(s, axis=1)


def rhs_of(s):
    y = jnp.concatenate(s, axis=1)
    return jnp.concatenate([y, y], axis=0)


def mm(a, b):
    o = dot(lhs_of(a), rhs_of(b))
    return o[:, :F] + o[:, F:]


def mm_two(a, c, b):
    o = dot(jnp.concatenate([lhs_of(a), lhs_of(c)], axis=0), rhs_of(b))
    o = o[:, :F] + o[:, F:]
    return o[:F], o[F:]


def mm_all(pairs):
    return [mm(a, b) for a, b in pairs]


def map_product(p, r):
    ph, pl_ = split(p)
    rh, rl = split(r)
    return dot(jnp.concatenate([ph, pl_], axis=1), jnp.concatenate([rh, rh], axis=0)) + dot(ph, rl)


HB = 4


def half_of(mine, w):
    return w[2] if mine else 1 - w[2]


def local_kernel(mine, w_ref, k_ref, v_ref, b_ref, map_ref, xh_ref, xl_ref, r_ref):
    g = pl.program_id(0)
    first_head = half_of(mine, w_ref) * 4 + g * HB
    beta_rows = b_ref[...]
    beta_cols = jnp.transpose(jnp.concatenate([beta_rows, jnp.zeros((F - HEADS, TOK), f32)], axis=0))
    lane = lax.broadcasted_iota(jnp.int32, (TOK, F), 1)
    row = lax.broadcasted_iota(jnp.int32, (F, F), 0)
    col = lax.broadcasted_iota(jnp.int32, (F, F), 1)
    eye = (row == col).astype(f32)
    strict = row > col
    in16 = jnp.logical_and(strict, (row // 16) == (col // 16))
    in64 = jnp.logical_and((row // 64) == (col // 64), (row // 16) > (col // 16))
    in128 = (row // 64) > (col // 64)

    stat = jnp.zeros((TOK, F), f32)
    ks, rs, bs, kraw = [], [], [], []
    for i in range(HB):
        k = k_ref[:, i * F:(i + 1) * F]
        kf = k.astype(f32)
        r = lax.rsqrt(jnp.sum(kf * kf, axis=-1, keepdims=True) + EPS)
        kf = jnp.where(r > 0.0, kf, 0.0)
        b = jnp.sum(jnp.where(lane == first_head + i, beta_cols, 0.0), axis=-1, keepdims=True)
        ks.append(kf)
        kraw.append(kf.astype(bf16))
        rs.append(r)
        bs.append(b)
        stat = jnp.where(lane == 2 * i, r, stat)
        stat = jnp.where(lane == 2 * i + 1, b, stat)
    stat_t = jnp.transpose(stat)
    r_ref[g] = stat_t[0:8, :]

    tiles = []
    cross = []
    for i in range(HB):
        r_row = stat_t[2 * i:2 * i + 1, :]
        br = bs[i] * rs[i]
        k1, k2 = kraw[i][:F], kraw[i][F:]
        g11 = dot_nt(k1, k1)
        g2 = dot_nt(k2, kraw[i])
        a11 = g11 * br[:F] * r_row[:, :F]
        a2 = g2 * br[F:] * r_row
        tiles += [a11, a2[:, F:]]
        cross.append(a2[:, :F])
    n = [jnp.where(in16, a, 0.0) for a in tiles]
    ns = [split(a) for a in n]
    n2 = mm_all(zip(ns, ns))
    n2s = [split(a) for a in n2]
    n4, q1 = zip(*[mm_two(b, a, b) for a, b in zip(ns, n2s)])
    n4s = [split(a) for a in n4]
    r1 = [eye - a + b - c for a, b, c in zip(n, n2, q1)]
    n8, q2 = zip(*[mm_two(b, split(a), b) for a, b in zip(r1, n4s)])
    r2 = [a + b for a, b in zip(r1, q2)]
    q3 = mm_all(zip([split(a) for a in r2], [split(a) for a in n8]))
    d = [a + b for a, b in zip(r2, q3)]
    ds = [split(a) for a in d]
    m = mm_all(zip(ds, [split(jnp.where(in64, a, 0.0)) for a in tiles]))
    ms = [split(a) for a in m]
    m2 = mm_all(zip(ms, ms))
    e = [a + b for a, b in zip(d, mm_all(zip([split(a) for a in m2], ds)))]
    t = [a - b for a, b in zip(e, mm_all(zip(ms, [split(a) for a in e])))]
    ts = [split(a) for a in t]
    u = mm_all(zip([split(jnp.where(in128, a, 0.0)) for a in tiles], ts))
    t = [a - b for a, b in zip(t, mm_all(zip(ts, [split(a) for a in u])))]
    ts = [split(a) for a in t]
    c1 = mm_all(zip([split(a) for a in cross], ts[0::2]))
    t21 = [-a for a in mm_all(zip(ts[1::2], [split(a) for a in c1]))]

    for i in range(HB):
        b_row = stat_t[2 * i + 1:2 * i + 2, :]
        t11h, t11l = split(t[2 * i] * b_row[:, :F])
        t2h, t2l = split(jnp.concatenate([t21[i], t[2 * i + 1]], axis=1) * b_row)
        kn = ks[i] * rs[i]
        knh, knl = split(kn)
        v = v_ref[:, i * F:(i + 1) * F]
        bh = jnp.concatenate([knh, v], axis=1)
        bh1 = bh[:F]
        x1 = dot(jnp.concatenate([t11h, t11l], axis=1), jnp.concatenate([bh1, bh1], axis=0))
        x2 = dot(t2h, bh) + dot(t2l, bh)
        y1 = dot(t11h, knl[:F])
        y2 = dot(t2h, knl)
        x = jnp.concatenate([x1, x2], axis=0)
        y = jnp.concatenate([y1, y2], axis=0)
        x = jnp.concatenate([x[:, :F] + y, x[:, F:]], axis=1)
        xh, xl = split(x)
        xh_ref[g * HB + i] = xh
        xl_ref[g * HB + i] = xl
        zh, zl = split(x * rs[i])
        pw = dot_tn(kraw[i], zh) + dot_tn(kraw[i], zl)
        map_ref[g * HB + i] = jnp.concatenate([eye - pw[:, :F], pw[:, F:]], axis=1)


def vmem(shape, dtype=f32):
    return pltpu.VMEM(shape, dtype)


PARAMS = pltpu.CompilerParams(vmem_limit_bytes=24 << 20)


def in_hbm(x):
    return pltpu.with_memory_space_constraint(x, pltpu.HBM)


def in_vmem(x):
    return pltpu.with_memory_space_constraint(x, pltpu.VMEM)


ANYV = pl.BlockSpec(memory_space=pltpu.VMEM)


def local_maps(mine, where, k, v, beta_rows):
    steps = 4 // HB
    cols = pl.BlockSpec((TOK, HB * F), lambda g, w: (0, half_of(mine, w) * steps + g))
    return pl.pallas_call(
        functools.partial(local_kernel, mine),
        grid_spec=pltpu.PrefetchScalarGridSpec(
            num_scalar_prefetch=1,
            grid=(steps,),
            in_specs=[cols, cols, pl.BlockSpec((HEADS, TOK), lambda g, w: (0, 0))],
            out_specs=[ANYV] * 4,
        ),
        out_shape=[
            vmem((4, F, 2 * F)),
            vmem((4, TOK, 2 * F), bf16),
            vmem((4, TOK, 2 * F), bf16),
            vmem((steps, 8, TOK)),
        ],
        compiler_params=PARAMS,
        name="local_maps",
    )(where, in_hbm(k), in_hbm(v), in_hbm(beta_rows))


def reads_kernel(w_ref, q_ref, k_ref, xh_ref, xl_ref, r_ref, m_ref, qh_ref, ql_ref, y_ref):
    g = pl.program_id(0)
    row = lax.broadcasted_iota(jnp.int32, (TOK, TOK), 0)
    col = lax.broadcasted_iota(jnp.int32, (TOK, TOK), 1)
    causal = row >= col
    for i in range(HB):
        q = q_ref[:, i * F:(i + 1) * F]
        k = k_ref[:, i * F:(i + 1) * F]
        r_row = r_ref[g, 2 * i:2 * i + 1, :]
        s = dot_nt(q, k) * r_row
        s = jnp.where(jnp.logical_and(causal, r_row > 0.0), s, 0.0)
        sh, sl = split(s)
        n = g * HB + i
        xh, xl = xh_ref[n], xl_ref[n]
        top = dot(jnp.concatenate([sh[:F, :F], sl[:F, :F]], axis=1), jnp.concatenate([xh[:F], xh[:F]], axis=0))
        top += dot(sh[:F, :F], xl[:F])
        o = jnp.concatenate([top, dot(sh[F:], xh) + (dot(sl[F:], xh) + dot(sh[F:], xl))], axis=0)
        qe = q.astype(f32) - o[:, :F]
        qh, ql = split(qe)
        qh_ref[n] = qh
        ql_ref[n] = ql
        y_ref[n] = o[:, F:]

        @pl.when(w_ref[2] == 1)
        def _():
            z = map_product(qe, m_ref[n])
            zh, zl = split(z[:, :F])
            qh_ref[n] = zh
            ql_ref[n] = zl
            y_ref[n] = o[:, F:] + z[:, F:]


def local_reads(mine, where, q, k, xh, xl, r, first):
    steps = 4 // HB
    cols = pl.BlockSpec((TOK, HB * F), lambda g, w: (0, half_of(mine, w) * steps + g))
    return pl.pallas_call(
        reads_kernel,
        grid_spec=pltpu.PrefetchScalarGridSpec(
            num_scalar_prefetch=1,
            grid=(steps,),
            in_specs=[cols, cols] + [ANYV] * 4,
            out_specs=[ANYV] * 3,
        ),
        out_shape=[vmem((4, TOK, F), bf16), vmem((4, TOK, F), bf16), vmem((4, TOK, F))],
        compiler_params=PARAMS,
        name="local_reads",
    )(where, in_hbm(q), in_hbm(k), *[in_vmem(a) for a in (xh, xl, r, first)])


def after(p_then, m):
    o = map_product(p_then[:, :F], m)
    return jnp.concatenate([o[:, :F], o[:, F:] + p_then[:, F:]], axis=1)


SHRINK = 1.0 / 32.0


def packed(m):
    return jnp.concatenate([m[:, :F], m[:, F:] * SHRINK], axis=1)


def unpacked(m):
    return jnp.concatenate([m[:, :F], m[:, F:] * (1.0 / SHRINK)], axis=1)


def stage(kernel, where, outs, *args, scratch=()):
    return pl.pallas_call(
        kernel,
        in_specs=[pl.BlockSpec(memory_space=pltpu.SMEM)] + [ANYV] * len(args),
        out_specs=[ANYV] * len(outs),
        out_shape=list(outs),
        scratch_shapes=list(scratch),
        compiler_params=PARAMS,
    )(where, *[in_vmem(a) for a in args])


def pair_kernel(w_ref, own_ref, got_ref, *out_refs):
    z, c = w_ref[1], w_ref[2]
    for k in range(4):
        j = lax.rem(z + k, 4)
        own = own_ref[j]
        got = got_ref[j]
        m = after(jnp.where(c == 0, got, own), jnp.where(c == 0, own, got))
        out_refs[k][...] = m if k == 0 else packed(m)


def chain_kernel(w_ref, m0_ref, m1_ref, m2_ref, m3_ref, pre_ref, all_ref, maps_ref):
    z = w_ref[1]
    for k, ref in enumerate((m0_ref, m1_ref, m2_ref, m3_ref)):
        maps_ref[lax.rem(z - k + 4, 4)] = ref[...] if k == 0 else unpacked(ref[...])
    m = maps_ref[0]
    pre_ref[0] = m
    for j in range(1, 4):
        m = after(maps_ref[j], m)
        if j < 3:
            pre_ref[j] = m
    all_ref[...] = packed(m)


def apply_map(m, s):
    return mm(split(m[:, :F]), split(s)) + m[:, F:]


def plane_kernel(w_ref, m3_ref, m2_ref, m1_ref, pre_ref, *out_refs):
    y, z = w_ref[0], w_ref[1]
    s = jnp.where(y >= 3, unpacked(m3_ref[...])[:, F:], 0.0)
    s = jnp.where(y >= 2, apply_map(unpacked(m2_ref[...]), s), 0.0)
    s = jnp.where(y >= 1, apply_map(unpacked(m1_ref[...]), s), 0.0)
    for k in range(4):
        j = lax.rem(z + k, 4)
        t = apply_map(pre_ref[jnp.maximum(j - 1, 0)], s)
        out_refs[k][...] = jnp.where(j == 0, s, t)


def order_kernel(w_ref, s0_ref, s1_ref, s2_ref, s3_ref, out_ref):
    z = w_ref[1]
    for k, ref in enumerate((s0_ref, s1_ref, s2_ref, s3_ref)):
        out_ref[lax.rem(z - k + 4, 4)] = ref[...]


def out_kernel(w_ref, qh_ref, ql_ref, y_ref, s_ref, g_ref, o_ref):
    mixed = [mm((qh_ref[i], ql_ref[i]), split(s_ref[i])) + y_ref[i] for i in range(4)]
    for i, m in enumerate(mixed):
        ms = jnp.mean(m * m, axis=-1, keepdims=True)
        o_ref[:, i * F:(i + 1) * F] = (m * lax.rsqrt(ms + EPS) * g_ref[...]).astype(bf16)


def outputs(where, qh, ql, y, s, gain):
    return stage(out_kernel, where, [vmem((TOK, 4 * F), bf16)], qh, ql, y, s, gain)[0]


def shift(x, axis, k):
    return lax.ppermute(x, axis, [(i, (i + k) % 4) for i in range(4)])


def swap(x, axis, k):
    n = 2 if axis == "core" else 4
    return lax.ppermute(x, axis, [(i, i ^ k) for i in range(n)])


def body(query_rows, key_rows, value_rows, beta, norm_gain, out_cotangent):
    yi, zi, ci, hi = (lax.axis_index(a).astype(jnp.int32) for a in ("y", "z", "core", "head"))
    where = jnp.stack([yi, zi, ci, hi])

    cot = lax.ppermute(out_cotangent, ("y", "head"), [(a * 4 + b, b * 4 + a) for a in range(4) for b in range(4)])
    cot1 = swap(cot, "head", 1)
    cot3 = swap(cot, "head", 3)
    t = TOK // 2
    top = swap(cot3[:t], "head", 1)
    low = swap(cot1[t:], "head", 3)
    cots = jnp.stack([cot, cot1, jnp.concatenate([top, low]), cot3])
    gain = norm_gain.reshape(1, F)
    beta_rows = beta.T
    m_a, xh_a, xl_a, r_a = local_maps(False, where, key_rows, value_rows, beta_rows)
    got_b = swap(m_a, "core", 1)
    m_b, xh_b, xl_b, r_b = local_maps(True, where, key_rows, value_rows, beta_rows)
    got_a = swap(m_b, "core", 1)
    m4 = vmem((F, 2 * F))
    comb = stage(pair_kernel, where, [m4] * 4, m_b, got_b)
    got = [comb[0]]
    for k in (1, 2, 3):
        got.append(shift(comb[k].astype(f16), "z", k).astype(f32))
    rd_b = local_reads(True, where, query_rows, key_rows, xh_b, xl_b, r_b, got_b)
    rd_a = local_reads(False, where, query_rows, key_rows, xh_a, xl_a, r_a, got_a)
    pre, total = stage(chain_kernel, where, [vmem((3, F, 2 * F)), m4], *got, scratch=[pltpu.VMEM((4, F, 2 * F), f32)])
    planes = []
    for k in (3, 2, 1):
        planes.append(shift(total.astype(f16), "y", k).astype(f32))
    sc = stage(plane_kernel, where, [vmem((F, F))] * 4, *planes, pre)
    sx = [sc[0]]
    for k in (1, 2, 3):
        sx.append(shift(sc[k], "z", k))
    s_b, = stage(order_kernel, where, [vmem((4, F, F))], *sx)
    s_a = swap(s_b, "core", 1)
    att_b = outputs(where, *rd_b, s_b, gain)
    up_b = shift(att_b, "y", 1)
    dn_b = shift(att_b, "y", -1)
    att_a = outputs(where, *rd_a, s_a, gain)
    up_a = shift(att_a, "y", 1)
    dn_a = shift(att_a, "y", -1)
    far_b = shift(up_b, "y", 1)
    far_a = shift(dn_a, "y", -1)

    parts = stage(part_kernel, where, [vmem((4 * F, 8 * F))] * 2, cots, att_b, att_a, up_b, up_a, dn_b, dn_a)
    w_send, = stage(functools.partial(last_kernel, 0), where, [vmem((4 * F, 8 * F), bf16)], cots, far_b, far_a, parts[0])
    w_got = swap(w_send, "core", 1)
    w, = stage(functools.partial(last_kernel, 1), where, [vmem((4 * F, 8 * F))], cots, far_b, far_a, parts[1])
    quarter = vmem((2 * F, 4 * F), bf16)
    kept = vmem((2 * F, 4 * F))
    on_b, on_a, k_b, k_a = stage(sum_kernel, where, [quarter, quarter, kept, kept], w, w_got)
    r_b = swap(on_b, "z", 1)
    r_a = swap(on_a, "z", 3)
    h_b = (k_b[F:] + r_b[F:].astype(f32)).astype(bf16)
    e_b = swap(h_b, "z", 3)
    h_a = (k_a[F:] + r_a[F:].astype(f32)).astype(bf16)
    e_a = swap(h_a, "z", 1)
    g_b = k_b[:F] + r_b[:F].astype(f32) + e_b.astype(f32)
    g_a = k_a[:F] + r_a[:F].astype(f32) + e_a.astype(f32)
    grad = jnp.where(ci == 0, jnp.concatenate([g_b, g_a], axis=1), jnp.concatenate([g_a, g_b], axis=1))
    attended = jnp.where(ci == 0, jnp.concatenate([att_b, att_a], axis=1), jnp.concatenate([att_a, att_b], axis=1))
    return attended, grad


def cot_rows(w_ref, cot_ref, k, part):
    d = lax.rem(w_ref[0] - k + 4, 4) ^ w_ref[3]
    j = d
    core = half_of(part == 1, w_ref)
    return jnp.concatenate(
        [cot_ref[j, :, pl.ds(pl.multiple_of((2 * n + core) * F, F), F)] for n in range(4)], axis=1
    )


def part_kernel(w_ref, cot_ref, *refs):
    for s in range(2):
        rows = jnp.concatenate([cot_rows(w_ref, cot_ref, k, s) for k in (0, 1, 3)], axis=0)
        for n in range(2):
            tall = jnp.concatenate([refs[n][...], refs[2 + n][...], refs[4 + n][...]], axis=0)
            refs[6 + s][:, n * 4 * F:(n + 1) * 4 * F] = dot_tn(rows, tall)


def last_kernel(s, w_ref, cot_ref, b_ref, a_ref, part_ref, out_ref):
    rows = cot_rows(w_ref, cot_ref, 2, s)
    for n, ref in enumerate((b_ref, a_ref)):
        cols = slice(n * 4 * F, (n + 1) * 4 * F)
        out_ref[:, cols] = (part_ref[:, cols] + dot_tn(rows, ref[...])).astype(out_ref.dtype)


def sum_kernel(w_ref, keep_ref, got_ref, on_b_ref, on_a_ref, k_b_ref, k_a_ref):
    z = w_ref[1]
    h = 4 * F
    for n, (on_ref, k_ref, first, second) in enumerate(((on_b_ref, k_b_ref, 1, 3), (on_a_ref, k_a_ref, 3, 1))):
        mine = slice(n * h, (n + 1) * h)
        theirs = slice((1 - n) * h, (2 - n) * h)
        for i, (ref, blk) in enumerate(((on_ref, z ^ first), (on_ref, z ^ 2), (k_ref, z), (k_ref, z ^ second))):
            rows = pl.ds(pl.multiple_of(blk * F, F), F)
            total = keep_ref[rows, mine] + got_ref[rows, theirs].astype(f32)
            ref[(i % 2) * F:(i % 2 + 1) * F, :] = total.astype(ref.dtype)


def solution(mesh):
    fine = Mesh(mesh.devices.reshape(4, 4, 2, 4), ("y", "z", "core", "head"))
    spec = P(("y", "z", "core"), "head")
    return jax.shard_map(
        body,
        mesh=fine,
        in_specs=(spec, spec, spec, spec, P(), spec),
        out_specs=(spec, spec),
        check_vma=False,
    )
```
